256 devices in a mesh: gx: 4 (over x), vert: 64 (over y, z, core).
Axes of the slice: x: 4, y: 4, z: 8, core: 2. Of those that a mesh axis runs over, the one named last changes fastest.
Arguments:
- dist: float32 [2, 4096, 24576], P(None, 'vert', 'gx'), may hold values from -6 to 6
- factors: float32 [2, 4096, 128], P(None, 'vert', 'gx'), may hold values from 0.95 to 0.999
- velocity: float32 [3, 2, 4096], P(None, None, 'vert'), may hold values from -3 to 3
- weights: float32 [13, 2, 4096], P(None, None, 'vert'), may hold values from -0.0625 to 0.0625
- relax: float32 [2, 4096], P(None, 'vert'), may hold values from 0.1 to 0.9
Outputs:
- updated: float32 [2, 4096, 24576], P(None, 'vert', 'gx')
- macro: float32 [13, 24576], P(None, 'gx')
The draws below stay inside these ranges and needn't reach their ends.
All inputs are finite; a program needn't handle non-finite values.
Results may differ from the reference program's by a relative error of at most 0.000071.
Values sent between devices are 32-bit elements; how exact they have to be, the bound alone decides.
A program may use at most 64 MiB of HBM per device.

```python
import math
import jax
import jax.numpy as jnp
from jax import lax

VEL = 4096
K = 13
SMOOTH = 4
YZ = 192
NX = 128
CELLS = 24576


def shard_levels(stream_key, dims, split, least, largest):
    level = 1.0
    for dim, blocks in split:
        steps = jax.random.uniform(jax.random.fold_in(jax.random.fold_in(stream_key, 6), dim), (blocks,), jnp.float32, least / len(split), largest / len(split))
        level = level * jnp.repeat(jnp.exp(steps), dims[dim] // blocks).reshape((-1,) + (1,) * (len(dims) - 1 - dim))
    return level


def scatter_about(key, extent, spread, reach, cuts=(), dtype=jnp.bfloat16):
    array = jax.random.normal(key, extent, jnp.float32) * spread
    if len(cuts) > 0:
        array = shard_levels(key, extent, cuts, -0.22, 0.18) * array
    return jnp.clip(array, min=-reach, max=reach).astype(dtype)


def setup_inputs(seed: int = 0) -> dict:
    arg_keys = jax.random.split(jax.random.key(seed), 6)
    return {
        "dist": scatter_about(arg_keys[0], (2, VEL, CELLS), 1.0, 6.0, ((1, 64), (2, 4)), jnp.float32),
        "factors": jnp.clip(jnp.exp(math.log(0.999) - 0.05029282 * jax.random.uniform(arg_keys[1], (2, VEL, NX), jnp.float32) ** shard_levels(arg_keys[1], (2, VEL, NX), ((1, 64), (2, 4)), -0.2, 0.2)), 0.95, 0.999),
        "velocity": jnp.clip(jax.random.uniform(arg_keys[2], (3, 2, VEL), jnp.float32, -3.0, 3.0) * shard_levels(arg_keys[2], (3, 2, VEL), ((2, 64),), -0.4, 0.0), -3.0, 3.0),
        "weights": scatter_about(arg_keys[3], (K, 2, VEL), (2 * VEL) ** -0.5, 0.0625, ((2, 64),), jnp.float32),
        "relax": jnp.clip(jnp.exp(math.log(0.9) - 2.1972245 * jax.random.uniform(arg_keys[4], (2, VEL), jnp.float32) ** shard_levels(arg_keys[4], (2, VEL), ((1, 64),), -0.2, 0.2)), 0.1, 0.9),
    }


smooth_rate = 0.24

def equilibrium(moments, speed_x, speed_y, speed_z):
    density = 1.0 + 0.5 * jnp.tanh(moments[0])
    flow_x = 0.5 * jnp.tanh(moments[1])
    flow_y = 0.5 * jnp.tanh(moments[2])
    flow_z = 0.5 * jnp.tanh(moments[3])
    temper = 1.0 + 0.5 * jnp.tanh(moments[4])
    stress = 0.2 * jnp.tanh(moments[5:10])
    fluxes = 0.2 * jnp.tanh(moments[10:13])
    rel_x = speed_x - flow_x
    rel_y = speed_y - flow_y
    rel_z = speed_z - flow_z
    square = rel_x * rel_x + rel_y * rel_y + rel_z * rel_z
    inverse = 1.0 / temper
    shape_term = stress[0] * rel_x * rel_y + stress[1] * rel_x * rel_z + stress[2] * rel_y * rel_z + 0.5 * stress[3] * (rel_x * rel_x - rel_z * rel_z) + 0.5 * stress[4] * (rel_y * rel_y - rel_z * rel_z)
    heat_term = (fluxes[0] * rel_x + fluxes[1] * rel_y + fluxes[2] * rel_z) * (0.5 * square * inverse - 2.5)
    return density * inverse * jnp.sqrt(inverse) * jnp.exp(-0.5 * square * inverse) * (1.0 + (shape_term + heat_term) * inverse)

def sweep_direction(rates, source, reverse):

    def advance(carry, item):
        rate, term = item
        value = rate[:, None] * carry + term
        return (value, value)
    start = jnp.zeros((source.shape[0], source.shape[2]), jnp.float32)
    _, values = lax.scan(advance, start, (rates.T, jnp.moveaxis(source, 1, 0)), reverse=reverse)
    return jnp.moveaxis(values, 0, 1)

def reference(dist, factors, velocity, weights, relax):
    grid = dist.reshape(2, VEL, NX, YZ)
    source = jnp.sqrt(1.0 - factors * factors)[..., None] * grid
    swept = jnp.stack([sweep_direction(factors[0], source[0], False), sweep_direction(factors[1], source[1], True)])
    moments = jnp.einsum('kdv,dvxc->kxc', weights, swept, precision=lax.Precision.HIGHEST)
    for step in range(SMOOTH):
        padded = jnp.pad(moments, ((0, 0), (1, 1), (0, 0)))
        coef = 1.0 / (1.0 + moments[0] * moments[0])
        moments = moments + smooth_rate * coef * (padded[:, 2:] - 2.0 * moments + padded[:, :-2])

    def relax_one(item):
        values, speeds, fraction = item
        equil = equilibrium(moments, speeds[0][:, None, None], speeds[1][:, None, None], speeds[2][:, None, None])
        return values + fraction[:, None, None] * (equil - values)
    result = lax.map(relax_one, (jnp.moveaxis(swept, 1, 0), jnp.moveaxis(velocity, 2, 0), relax.T))
    updated = jnp.moveaxis(result, 0, 1).reshape(2, VEL, NX * YZ)
    return (updated, moments.reshape(K, NX * YZ))
```

```python
import functools

import jax
import jax.numpy as jnp
from jax import lax
from jax.experimental import pallas as pl
from jax.experimental.pallas import tpu as pltpu
from jax.sharding import PartitionSpec as P

MESH = pl.DeviceIdType.MESH
F32, BF16 = jnp.float32, jnp.bfloat16
SMOOTH_RATE = 0.24
LOG2E = 1.4426950408889634

NX, NY, NZ = 4, 4, 8
TILES, SLOT = 48, 6
SLOT_ROWS = SLOT * 16
GROUPS = 2

XF, CR = 0, 6 * GROUPS
YR = CR + 4
ZR = YR + 3
ZG = ZR + 7
YG = ZG + 7
CG = YG + 3
HALO = CG + 5
N_SEM = HALO + 4


def kernel(
    dist, fac, vel, wgt, rel, out, mac,
    val, reach, snd, rcv, inc, wmat, phi, phit, coef_f, coef_l,
    stage, part, got_c, got_y, got_z, full, tmp, ld_sem, st_sem, ssem, rsem,
):
    gx = lax.axis_index("gx")
    vert = lax.axis_index("vert")
    y = vert // 16
    z = (vert // 2) % 8
    core = vert % 2

    def vert_of(y_, z_, core_):
        return y_ * 16 + z_ * 2 + core_

    def copy(src, dst, send, recv, x_, v_):
        return pltpu.make_async_remote_copy(
            src_ref=src, dst_ref=dst, send_sem=ssem.at[send], recv_sem=rsem.at[recv],
            device_id=(x_, v_), device_id_type=MESH,
        )

    def rows8(r):
        return pl.ds(pl.multiple_of(r * 8, 8), 8)

    def load(r):
        return pltpu.make_async_copy(dist.at[:, rows8(r), :], val.at[:, rows8(r), :], ld_sem.at[r])

    for r in range(8):
        load(r).start()

    barrier = pltpu.get_barrier_semaphore()

    def greet(x_, v_):
        pl.semaphore_signal(barrier, inc=1, device_id=(x_, v_), device_id_type=MESH)

    for t in range(1, NX):
        greet((gx + t) % NX, vert)
    greet(gx, vert_of(y, z, 1 - core))
    for t in range(1, NY):
        greet(gx, vert_of((y + t) % NY, z, core))
    for t in range(1, NZ):
        greet(gx, vert_of(y, (z + t) % NZ, core))
    has_left, has_right = gx > 0, gx < NX - 1
    halo_here = jnp.where(core == 1, has_left, has_right)
    halo_x = jnp.where(core == 1, gx - 1, gx + 1)
    halo_y = jnp.where(core == 1, NY - 1, 0)

    @pl.when(halo_here & (y != halo_y))
    def _():
        greet(halo_x, vert_of(halo_y, z, core))

    halo_source = ((core == 1) & (y == NY - 1) & has_right) | ((core == 0) & (y == 0) & has_left)

    lane = lax.broadcasted_iota(jnp.int32, (8, 128), 1)
    low = lane < 64

    def lanes2(a, b):
        return jnp.concatenate([a, b], axis=1)

    wide = jnp.zeros((16, 128), F32)
    wmat[...] = jnp.zeros_like(wmat)
    for k in range(13):
        row = lanes2(wgt[k, 0:1, :], wgt[k, 1:2, :])
        hi = row.astype(BF16).astype(F32)
        lo = row - hi
        wmat[k : k + 1, 0:128] = hi
        wmat[k : k + 1, 128:256] = hi
        wmat[16 + k : 17 + k, 0:128] = lo

    vx, vy, vz = [lanes2(vel[j, 0:1, :], vel[j, 1:2, :]) for j in range(3)]
    relax = lanes2(rel[0:1, :], rel[1:2, :])
    xx, yy, zz = vx * vx, vy * vy, vz * vz
    sq = xx + yy + zz
    one = jnp.ones_like(vx)
    feats = [vx * sq, vy * sq, vz * sq, xx, yy, zz, vx * vy, vx * vz, vy * vz, vx, vy, vz, one]
    phi[...] = jnp.zeros_like(phi)
    for n, feat in enumerate(feats):
        for base, f in ((0, feat * relax), (48, feat)):
            hi = f.astype(BF16).astype(F32)
            phi[base + n : base + n + 1, :] = hi
            phi[base + 16 + n : base + 17 + n, :] = hi
            phi[base + 32 + n : base + 33 + n, :] = f - hi
    phi[96:97, :] = 1.0 - relax
    phit[...] = phi[...].T

    def sweep(r, direction):
        rows = rows8(r)
        f = fac[direction, rows, :]
        q = jnp.sqrt(1.0 - f * f)

        def cols(t):
            return pl.ds(t * 128, 128)

        def spread(x, i):
            return jnp.broadcast_to(x[:, i : i + 1], (8, 128))

        zero = jnp.zeros((8, 128), F32)
        ones = jnp.ones((8, 128), F32)
        if direction == 0:
            f_prev = ones
            roll_a = roll_b = zero
            value = [zero] * 3
            total = [ones] * 3
            for p in range(16):
                fa, fc = spread(f, 2 * p), spread(f, 2 * p + 1)
                qa, qc = spread(q, 2 * p), spread(q, 2 * p + 1)
                ga, gc = fa * f_prev, fc * fa
                fs = [fa, jnp.where(low, fa, fc), fc]
                qs = [qa, jnp.where(low, qa, qc), qc]
                gs = [ga, jnp.where(low, ga, gc), gc]
                for j in range(3):
                    t = 3 * p + j
                    s = qs[j] * val[0, rows, cols(t)]
                    before = jnp.where(low, roll_a, roll_b)
                    roll_a, roll_b = roll_b, pltpu.roll(s, 64, 1)
                    value[j] = gs[j] * value[j] + (s + fs[j] * before)
                    total[j] = gs[j] * total[j]
                    val[0, rows, cols(t)] = value[j]
                    reach[0, rows, cols(t)] = total[j]
                f_prev = fc
            snd[0, rows, 0:128] = jnp.where(low, total[2], value[1])
            snd[0, rows, 128:256] = value[2]
        else:
            f_next = ones
            roll_a = roll_b = zero
            value = [zero] * 3
            total = [ones] * 3
            for p in range(15, -1, -1):
                fa, fc = spread(f, 2 * p), spread(f, 2 * p + 1)
                qa, qc = spread(q, 2 * p), spread(q, 2 * p + 1)
                ga, gc = fa * fc, fc * f_next
                fs = [fa, jnp.where(low, fa, fc), fc]
                qs = [qa, jnp.where(low, qa, qc), qc]
                gs = [ga, jnp.where(low, ga, gc), gc]
                for j in (2, 1, 0):
                    t = 3 * p + j
                    s = qs[j] * val[1, rows, cols(t)]
                    after = jnp.where(low, roll_b, roll_a)
                    roll_a, roll_b = roll_b, pltpu.roll(s, 64, 1)
                    value[j] = gs[j] * value[j] + (s + fs[j] * after)
                    total[j] = gs[j] * total[j]
                    val[1, rows, cols(t)] = value[j]
                    reach[1, rows, cols(t)] = total[j]
                f_next = fa
            snd[1, rows, 0:128] = value[0]
            snd[1, rows, 128:256] = jnp.where(low, value[1], total[0])

    def edge(direction, t, g, target):
        span = pl.ds(g * (64 // GROUPS), 64 // GROUPS)
        n = XF + (direction * 3 + t - 1) * GROUPS + g
        return copy(snd.at[direction, span, :], rcv.at[direction, t - 1, span, :], n, n, target, vert)

    for g in range(GROUPS):
        def sweep_rows(r, _):
            load(r).wait()
            sweep(r, 0)
            sweep(r, 1)
            return 0

        lax.fori_loop(g * 8 // GROUPS, (g + 1) * 8 // GROUPS, sweep_rows, 0)
        if g == 0:
            pl.semaphore_wait(barrier, 14 + jnp.where(halo_source, 3, 0))

        for t in range(1, NX):
            @pl.when(gx + t < NX)
            def _():
                edge(0, t, g, gx + t).start()

            @pl.when(gx - t >= 0)
            def _():
                edge(1, t, g, gx - t).start()

    for t in range(1, NX):
        for g in range(GROUPS):
            @pl.when(gx - t >= 0)
            def _():
                edge(0, t, g, (gx - t) % NX).wait_recv()

            @pl.when(gx + t < NX)
            def _():
                edge(1, t, g, (gx + t) % NX).wait_recv()

    def enter(r, _):
        rows = rows8(r)
        zero = jnp.zeros((8, 128), F32)

        def forward(n, state):
            a, b = state
            ra, rb = rcv[0, gx - n - 1, rows, 0:128], rcv[0, gx - n - 1, rows, 128:256]
            through = jnp.broadcast_to(ra[:, 0:1], (8, 128))
            return through * a + ra, through * b + rb

        a, b = lax.fori_loop(0, gx, forward, (zero, zero))
        ra, rb = pltpu.roll(a, 64, 1), pltpu.roll(b, 64, 1)
        inc[0, rows, 0:128] = jnp.where(low, ra, rb)
        inc[0, rows, 128:256] = jnp.where(low, rb, a)
        inc[0, rows, 256:384] = b

        def backward(n, state):
            a, b = state
            last = NX - 2 - gx - n
            ra, rb = rcv[1, last, rows, 0:128], rcv[1, last, rows, 128:256]
            through = jnp.broadcast_to(rb[:, 127:128], (8, 128))
            return through * a + ra, through * b + rb

        a, b = lax.fori_loop(0, NX - 1 - gx, backward, (zero, zero))
        ra, rb = pltpu.roll(a, 64, 1), pltpu.roll(b, 64, 1)
        inc[1, rows, 0:128] = a
        inc[1, rows, 128:256] = jnp.where(low, b, ra)
        inc[1, rows, 256:384] = jnp.where(low, ra, rb)
        return 0

    lax.fori_loop(0, 8, enter, 0)

    weights = wmat[...].astype(BF16)

    def moments(slot, dst, dst_row):
        for half in range(2):
            cols = pl.ds(pl.multiple_of(slot * 768 + half * 384, 128), 384)
            swept = val[:, :, cols] + reach[:, :, cols] * inc[...]
            val[:, :, cols] = swept
            flat = swept.reshape(128, 384)
            hi = flat.astype(BF16)
            lo = (flat - hi.astype(F32)).astype(BF16)
            both = jnp.dot(weights, jnp.concatenate([hi, lo], axis=0), preferred_element_type=F32)
            total = both[0:16] + both[16:32]
            for j in range(3):
                dst[pl.ds(pl.multiple_of(dst_row + (half * 3 + j) * 16, 16), 16), :] = total[:, j * 128 : (j + 1) * 128]

    def slot_rows(n):
        return pl.ds(pl.multiple_of(n * SLOT_ROWS, SLOT_ROWS), SLOT_ROWS)

    partner = vert_of(y, z, 1 - core)

    def to_core(n):
        return copy(stage.at[slot_rows(n), :], got_c.at[slot_rows(n), :], CR + n, CR + n, gx, partner)

    def other_half(n, _):
        moments((1 - core) * 4 + (y + n + 1) % NY, stage, n * SLOT_ROWS)
        to_core(n).start()
        return 0

    lax.fori_loop(0, 4, other_half, 0)

    def to_y(n):
        return copy(
            part.at[slot_rows(n), :], got_y.at[slot_rows(n), :], YR + n, YR + n, gx, vert_of((y + n + 1) % NY, z, core)
        )

    def own_half(n, _):
        moments(core * 4 + (y + n + 1) % NY, part, n * SLOT_ROWS)
        to_core(n).wait_recv()
        part[slot_rows(n), :] += got_c[slot_rows(n), :]

        @pl.when(n < 3)
        def _():
            to_y(n).start()

        return 0

    lax.fori_loop(0, 4, own_half, 0)
    for n in range(3):
        to_y(n).wait_recv()
        part[slot_rows(3), :] += got_y[slot_rows(n), :]

    def tile_rows(n):
        return pl.ds(pl.multiple_of(n * 16, 16), 16)

    mine = core * 4 + y
    own_row = (1 + mine) * SLOT_ROWS

    def to_z(n):
        peer = (z + n + 1) % NZ
        return copy(
            part.at[pl.ds(pl.multiple_of(3 * SLOT_ROWS + peer * 16, 16), 16), :], got_z.at[tile_rows(n), :],
            ZR + n, ZR + n, gx, vert_of(y, peer, core),
        )

    def from_owner(n, owner, target):
        tile = pl.ds(pl.multiple_of(own_row + owner * 16, 16), 16)
        return copy(full.at[tile, :], full.at[tile, :], ZG + n, ZG + n, gx, vert_of(y, target, core))

    for n in range(7):
        @pl.when((z + n + 1) % NZ < SLOT)
        def _():
            to_z(n).start()

    @pl.when(z < SLOT)
    def _():
        total = part[pl.ds(pl.multiple_of(3 * SLOT_ROWS + z * 16, 16), 16), :]
        for n in range(7):
            copy(got_z.at[tile_rows(n), :], got_z.at[tile_rows(n), :], ZR + n, ZR + n, gx, vert).wait_recv()
            total += got_z[tile_rows(n), :]
        full[pl.ds(pl.multiple_of(own_row + z * 16, 16), 16), :] = total
        for n in range(7):
            from_owner(n, z, (z + n + 1) % NZ).start()

    for n in range(7):
        owner = (z + NZ - n - 1) % NZ

        @pl.when(owner < SLOT)
        def _():
            from_owner(n, owner, z).wait_recv()

    def slot_of(n):
        return pl.ds(pl.multiple_of((1 + n) * SLOT_ROWS, SLOT_ROWS), SLOT_ROWS)

    def gather_y(n, slot):
        return copy(
            full.at[slot_of(slot), :], full.at[slot_of(slot), :], YG + n, YG + n, gx, vert_of((y + n + 1) % NY, z, core)
        )

    halo_slot = jnp.where(core == 1, -1, 8)

    def send_halo(n):
        return copy(
            full.at[slot_of(mine), :], full.at[slot_of(halo_slot), :], HALO + n, HALO,
            jnp.where(core == 1, gx + 1, gx - 1), vert_of((y + n) % NY, z, core),
        )

    def gather_core(n, slot):
        return copy(full.at[slot_of(slot), :], full.at[slot_of(slot), :], CG + n, CG + n, gx, partner)

    for n in range(3):
        gather_y(n, mine).start()

    @pl.when(halo_source)
    def _():
        for n in range(4):
            send_halo(n).start()

    gather_core(3, mine).start()
    for n in range(3):
        slot = core * 4 + (y + NY - n - 1) % NY
        gather_y(n, slot).wait_recv()
        gather_core(n, slot).start()

    @pl.when(halo_here)
    def _():
        copy(full.at[slot_of(halo_slot), :], full.at[slot_of(halo_slot), :], HALO, HALO, gx, vert).wait_recv()
        gather_core(4, halo_slot).start()

    nothing = jnp.zeros((SLOT_ROWS, 128), F32)

    @pl.when(jnp.logical_not(has_left))
    def _():
        full[slot_of(-1), :] = nothing

    @pl.when(jnp.logical_not(has_right))
    def _():
        full[slot_of(8), :] = nothing

    for n in range(4):
        gather_core(n, (1 - core) * 4 + (y + NY - n - 1) % NY).wait_recv()

    other_halo = jnp.where(core == 1, 8, -1)

    @pl.when(jnp.where(core == 1, has_right, has_left))
    def _():
        gather_core(4, other_halo).wait_recv()

    for n in range(3):
        gather_y(n, mine).wait_send()

    @pl.when(halo_source)
    def _():
        for n in range(4):
            send_halo(n).wait_send()

    for n in range(4):
        gather_core(n, core * 4 + (y + NY - n - 1) % NY).wait_send()

    @pl.when(halo_here)
    def _():
        gather_core(4, halo_slot).wait_send()

    @pl.when(z < SLOT)
    def _():
        for n in range(7):
            from_owner(n, z, (z + n + 1) % NZ).wait_send()

    left_flag = jnp.where(has_left, 1.0, 0.0).astype(F32)
    right_flag = jnp.where(has_right, 1.0, 0.0).astype(F32)

    def smooth(src, dst, first, last):
        def get(t):
            if t < 0 or t > 59:
                return [jnp.zeros((8, 128), F32)] * 2
            return [src[t * 16 + 8 * h : t * 16 + 8 * h + 8, :] for h in range(2)]

        def rolled(t):
            return [pltpu.roll(m, 64, 1) for m in get(t)]

        around = {t: rolled(t) for t in range(first - 2, first + 2)}
        for t in range(first, last + 1):
            around[t + 2] = rolled(t + 2)
            here = get(t)
            density = jnp.broadcast_to(here[0][0:1, :], (8, 128))
            coef = SMOOTH_RATE / (1.0 + density * density)
            if t < SLOT:
                coef = coef * left_flag
            if t >= 54:
                coef = coef * right_flag
            for h in range(2):
                before = jnp.where(low, around[t - 2][h], around[t - 1][h])
                after = jnp.where(low, around[t + 1][h], around[t + 2][h])
                dst[t * 16 + 8 * h : t * 16 + 8 * h + 8, :] = here[h] + coef * (before + after - 2.0 * here[h])
            del around[t - 2]

    smooth(full, tmp, 1, 58)
    smooth(tmp, full, 3, 56)
    smooth(full, tmp, 4, 55)
    smooth(tmp, full, 6, 53)
    for t in range(TILES):
        mac[:, t * 128 : (t + 1) * 128] = full[(t + 6) * 16 : (t + 6) * 16 + 13, :]

    def row(k):
        return jnp.tanh(full[pl.ds(96 + k, TILES, stride=16), :])

    density = 1.0 + 0.5 * row(0)
    ux, uy, uz = 0.5 * row(1), 0.5 * row(2), 0.5 * row(3)
    g = 1.0 / (1.0 + 0.5 * row(4))
    s0, s1, s2, s3, s4 = [0.2 * row(5 + j) for j in range(5)]
    qx, qy, qz = [0.2 * row(10 + j) for j in range(3)]
    front = density * g * jnp.sqrt(g)
    h = 0.5 * g
    sxx, syy = 0.5 * s3, 0.5 * s4
    szz = -(sxx + syy)
    square = ux * ux + uy * uy + uz * uz
    a = qx * ux + qy * uy + qz * uz
    b = h * square - 2.5
    ah = a * h
    scale = front * g
    quad = (
        ux * (sxx * ux + s0 * uy + s1 * uz) + uy * (syy * uy + s2 * uz) + szz * uz * uz
    )
    values_f = [
        scale * h * qx, scale * h * qy, scale * h * qz,
        scale * (sxx - g * qx * ux - ah),
        scale * (syy - g * qy * uy - ah),
        scale * (szz - g * qz * uz - ah),
        scale * (s0 - g * (qx * uy + qy * ux)),
        scale * (s1 - g * (qx * uz + qz * ux)),
        scale * (s2 - g * (qy * uz + qz * uy)),
        scale * (b * qx + 2.0 * ah * ux - (2.0 * sxx * ux + s0 * uy + s1 * uz)),
        scale * (b * qy + 2.0 * ah * uy - (s0 * ux + 2.0 * syy * uy + s2 * uz)),
        scale * (b * qz + 2.0 * ah * uz - (s1 * ux + s2 * uy + 2.0 * szz * uz)),
        front + scale * (quad - a * b),
    ]
    le = -LOG2E * h
    none = jnp.zeros_like(le)
    values_l = [none] * 3 + [le] * 3 + [none] * 3 + [-2.0 * le * ux, -2.0 * le * uy, -2.0 * le * uz, le * square]
    for n in range(16):
        coef_f[pl.ds(n, TILES, stride=16), :] = values_f[n] if n < 13 else none
        coef_l[pl.ds(n, TILES, stride=16), :] = values_l[n] if n < 13 else none

    lhs_f = phit[:, 0:48].astype(BF16)
    lhs_l = phit[:, 48:96].astype(BF16)
    keep = jnp.broadcast_to(phit[:, 96:97], (128, 128))
    keep = jnp.concatenate([keep] * 3, axis=1)

    def split(ref, n):
        c = jnp.concatenate([ref[pl.ds(pl.multiple_of(n * 48 + 16 * j, 16), 16), :] for j in range(3)], axis=1)
        hi = c.astype(BF16)
        lo = (c - hi.astype(F32)).astype(BF16)
        return jnp.concatenate([hi, lo, hi], axis=0)

    def relaxed(n, _):
        cols = pl.ds(pl.multiple_of(n * 384, 128), 384)
        poly = jnp.dot(lhs_f, split(coef_f, n), preferred_element_type=F32)
        power = jnp.dot(lhs_l, split(coef_l, n), preferred_element_type=F32)
        swept = val[:, :, cols].reshape(128, 384)
        out[:, :, cols] = (keep * swept + poly * jnp.exp2(power)).reshape(2, 64, 384)
        return 0

    lax.fori_loop(0, 16, relaxed, 0)

    for g in range(GROUPS):
        for t in range(1, NX):
            @pl.when(gx + t < NX)
            def _():
                edge(0, t, g, (gx + t) % NX).wait_send()

            @pl.when(gx - t >= 0)
            def _():
                edge(1, t, g, (gx - t) % NX).wait_send()

    for n in range(4):
        to_core(n).wait_send()
    for n in range(3):
        to_y(n).wait_send()
    for n in range(7):
        @pl.when((z + n + 1) % NZ < SLOT)
        def _():
            to_z(n).wait_send()


def per_device(dist, factors, velocity, weights, relax):
    vmem = pl.BlockSpec(memory_space=pltpu.VMEM)
    return pl.pallas_call(
        kernel,
        out_shape=(
            jax.ShapeDtypeStruct((2, 64, 6144), F32),
            jax.ShapeDtypeStruct((13, 6144), F32),
        ),
        in_specs=[pl.BlockSpec(memory_space=pl.ANY), vmem, vmem, vmem, vmem],
        out_specs=(vmem, vmem),
        scratch_shapes=[
            pltpu.VMEM((2, 64, 6144), F32),
            pltpu.VMEM((2, 64, 6144), F32),
            pltpu.VMEM((2, 64, 256), F32),
            pltpu.VMEM((2, 3, 64, 256), F32),
            pltpu.VMEM((2, 64, 384), F32),
            pltpu.VMEM((32, 256), F32),
            pltpu.VMEM((128, 128), F32),
            pltpu.VMEM((128, 128), F32),
            pltpu.VMEM((TILES * 16, 128), F32),
            pltpu.VMEM((TILES * 16, 128), F32),
            pltpu.VMEM((4 * SLOT_ROWS, 128), F32),
            pltpu.VMEM((4 * SLOT_ROWS, 128), F32),
            pltpu.VMEM((4 * SLOT_ROWS, 128), F32),
            pltpu.VMEM((3 * SLOT_ROWS, 128), F32),
            pltpu.VMEM((7 * 16, 128), F32),
            pltpu.VMEM((10 * SLOT_ROWS, 128), F32),
            pltpu.VMEM((10 * SLOT_ROWS, 128), F32),
            pltpu.SemaphoreType.DMA((8,)),
            pltpu.SemaphoreType.DMA((8,)),
            pltpu.SemaphoreType.DMA((N_SEM,)),
            pltpu.SemaphoreType.DMA((N_SEM,)),
        ],
        compiler_params=pltpu.CompilerParams(
            collective_id=0, has_side_effects=True, vmem_limit_bytes=32 * 2**20
        ),
    )(dist, factors, velocity, weights, relax)


def solution(mesh):
    return jax.shard_map(
        per_device,
        mesh=mesh,
        in_specs=(
            P(None, "vert", "gx"),
            P(None, "vert", "gx"),
            P(None, None, "vert"),
            P(None, None, "vert"),
            P(None, "vert"),
        ),
        out_specs=(P(None, "vert", "gx"), P(None, "gx")),
        check_vma=False,
    )
```

```python
import functools

import jax
import jax.numpy as jnp
from jax import lax
from jax.experimental import pallas as pl
from jax.experimental.pallas import tpu as pltpu
from jax.sharding import PartitionSpec as P

MESH = pl.DeviceIdType.MESH
F32, BF16 = jnp.float32, jnp.bfloat16
SMOOTH_RATE = 0.24
LOG2E = 1.4426950408889634

NX, NY, NZ = 4, 4, 8
TILES, SLOT = 48, 6
SLOT_ROWS = SLOT * 16
GROUPS = 2
BUFS = 4

XF, CR = 0, 6 * GROUPS
YR = CR + 4
ZR = YR + 3
ZG = ZR + 7
YG = ZG + 7
CG = YG + 3
HALO = CG + 5
N_SEM = HALO + 4


def kernel(
    dist, fac_hbm, vel_hbm, wgt_hbm, rel_hbm, val, moved, phit,
    fac, vel, wgt, rel, lhs, reach, scaled, snd, rcv, inc, wmat, phi,
    stage, part, got_c, got_y, got_z, full, tmp, ld_sem, small_sem, ssem, rsem,
):
    gx = lax.axis_index("gx")
    vert = lax.axis_index("vert")
    y = vert // 16
    z = (vert // 2) % 8
    core = vert % 2

    def vert_of(y_, z_, core_):
        return y_ * 16 + z_ * 2 + core_

    def copy(src, dst, send, recv, x_, v_):
        return pltpu.make_async_remote_copy(
            src_ref=src, dst_ref=dst, send_sem=ssem.at[send], recv_sem=rsem.at[recv],
            device_id=(x_, v_), device_id_type=MESH,
        )

    def rows8(r):
        return pl.ds(pl.multiple_of(r * 8, 8), 8)

    def load(r):
        return pltpu.make_async_copy(dist.at[:, rows8(r), :], val.at[:, rows8(r), :], ld_sem.at[r])

    small = [
        pltpu.make_async_copy(src, dst, small_sem.at[n])
        for n, (src, dst) in enumerate(((fac_hbm, fac), (wgt_hbm, wgt), (vel_hbm, vel), (rel_hbm, rel)))
    ]
    for one_copy in small:
        one_copy.start()
    for r in range(8):
        load(r).start()

    barrier = pltpu.get_barrier_semaphore()

    def greet(x_, v_):
        pl.semaphore_signal(barrier, inc=1, device_id=(x_, v_), device_id_type=MESH)

    for t in range(1, NX):
        greet((gx + t) % NX, vert)
    greet(gx, vert_of(y, z, 1 - core))
    for t in range(1, NY):
        greet(gx, vert_of((y + t) % NY, z, core))
    for t in range(1, NZ):
        greet(gx, vert_of(y, (z + t) % NZ, core))
    has_left, has_right = gx > 0, gx < NX - 1
    halo_here = jnp.where(core == 1, has_left, has_right)
    halo_x = jnp.where(core == 1, gx - 1, gx + 1)
    halo_y = jnp.where(core == 1, NY - 1, 0)

    @pl.when(halo_here & (y != halo_y))
    def _():
        greet(halo_x, vert_of(halo_y, z, core))

    halo_source = ((core == 1) & (y == NY - 1) & has_right) | ((core == 0) & (y == 0) & has_left)

    lane = lax.broadcasted_iota(jnp.int32, (8, 128), 1)
    low = lane < 64

    def lanes2(a, b):
        return jnp.concatenate([a, b], axis=1)

    small[0].wait()
    compact = lanes2(fac[0], fac[1])
    for n, x in enumerate((compact, jnp.sqrt(1.0 - compact * compact))):
        hi = x.astype(BF16).astype(F32)
        mid = (x - hi).astype(BF16).astype(F32)
        parts = jnp.concatenate([hi, mid, x - hi - mid, jnp.zeros_like(x)], axis=0)
        lhs[n * 128 : (n + 1) * 128, :] = parts.T.astype(BF16)

    def spread(p, _):
        cell = lax.broadcasted_iota(jnp.int32, (96, 384), 0) % 32
        second = lax.broadcasted_iota(jnp.int32, (96, 384), 1) >= 192
        picks = jnp.where(cell == 2 * p + jnp.where(second, 1, 0), 1.0, 0.0).astype(BF16)
        cols = pl.ds(pl.multiple_of(p * 384, 128), 384)
        both = jnp.dot(lhs[:, 0:96], picks, preferred_element_type=F32)
        reach[:, :, cols] = both[0:128].reshape(2, 64, 384)
        scaled[:, :, cols] = both[128:256].reshape(2, 64, 384)
        return 0

    lax.fori_loop(0, 16, spread, 0)

    def sweep(r):
        rows = rows8(r)
        zero = jnp.zeros((8, 128), F32)
        ones = jnp.ones((8, 128), F32)

        def cols(t):
            return pl.ds(t * 128, 128)

        value = [[zero] * 3, [zero] * 3]
        total = [[ones] * 3, [ones] * 3]
        rolls = [[zero, zero], [zero, zero]]
        f_near = [ones, ones]
        for step in range(16):
            for d in range(2):
                p = step if d == 0 else 15 - step
                f = [reach[d, rows, cols(3 * p + j)] for j in range(3)]
                first, second = (f[0], f[2]) if d == 0 else (f[2], f[0])
                near, far = first * f_near[d], second * first
                f_near[d] = second
                if d == 0:
                    gs = [near, jnp.where(low, near, far), far]
                else:
                    gs = [far, jnp.where(low, far, near), near]
                for j in (0, 1, 2) if d == 0 else (2, 1, 0):
                    t = 3 * p + j
                    s = scaled[d, rows, cols(t)] * val[d, rows, cols(t)]
                    two_off, one_off = rolls[d]
                    neighbour = jnp.where(low, two_off, one_off) if d == 0 else jnp.where(low, one_off, two_off)
                    rolls[d] = [one_off, pltpu.roll(s, 64, 1)]
                    value[d][j] = gs[j] * value[d][j] + (s + f[j] * neighbour)
                    total[d][j] = gs[j] * total[d][j]
                    val[d, rows, cols(t)] = value[d][j]
                    reach[d, rows, cols(t)] = total[d][j]
        snd[0, rows, 0:128] = jnp.where(low, total[0][2], value[0][1])
        snd[0, rows, 128:256] = value[0][2]
        snd[1, rows, 0:128] = value[1][0]
        snd[1, rows, 128:256] = jnp.where(low, value[1][1], total[1][0])

    def edge(direction, t, g, target):
        span = pl.ds(g * (64 // GROUPS), 64 // GROUPS)
        n = XF + (direction * 3 + t - 1) * GROUPS + g
        return copy(snd.at[direction, span, :], rcv.at[direction, t - 1, span, :], n, n, target, vert)

    def drain_x():
        for g in range(GROUPS):
            for t in range(1, NX):
                @pl.when(gx + t < NX)
                def _():
                    edge(0, t, g, (gx + t) % NX).wait_send()

                @pl.when(gx - t >= 0)
                def _():
                    edge(1, t, g, (gx - t) % NX).wait_send()

    for g in range(GROUPS):
        def sweep_rows(r, _):
            load(r).wait()
            sweep(r)
            return 0

        lax.fori_loop(g * 8 // GROUPS, (g + 1) * 8 // GROUPS, sweep_rows, 0)
        if g == 0:
            pl.semaphore_wait(barrier, 14 + jnp.where(halo_source, 3, 0))

        for t in range(1, NX):
            @pl.when(gx + t < NX)
            def _():
                edge(0, t, g, gx + t).start()

            @pl.when(gx - t >= 0)
            def _():
                edge(1, t, g, gx - t).start()

    for one_copy in small[1:]:
        one_copy.wait()
    wmat[...] = jnp.zeros_like(wmat)
    for k in range(13):
        row = lanes2(wgt[k, 0:1, :], wgt[k, 1:2, :])
        hi = row.astype(BF16).astype(F32)
        lo = row - hi
        wmat[k : k + 1, 0:128] = hi
        wmat[k : k + 1, 128:256] = hi
        wmat[16 + k : 17 + k, 0:128] = lo

    vx, vy, vz = [lanes2(vel[j, 0:1, :], vel[j, 1:2, :]) for j in range(3)]
    relax = lanes2(rel[0:1, :], rel[1:2, :])
    xx, yy, zz = vx * vx, vy * vy, vz * vz
    sq = xx + yy + zz
    one = jnp.ones_like(vx)
    feats = [vx * sq, vy * sq, vz * sq, xx, yy, zz, vx * vy, vx * vz, vy * vz, vx, vy, vz, one]
    phi[...] = jnp.zeros_like(phi)
    for n, feat in enumerate(feats):
        for base, f in ((0, feat * relax), (48, feat)):
            hi = f.astype(BF16).astype(F32)
            phi[base + n : base + n + 1, :] = hi
            phi[base + 16 + n : base + 17 + n, :] = hi
            phi[base + 32 + n : base + 33 + n, :] = f - hi
    phi[96:97, :] = 1.0 - relax
    phit[...] = phi[...].T

    for t in range(1, NX):
        for g in range(GROUPS):
            @pl.when(gx - t >= 0)
            def _():
                edge(0, t, g, (gx - t) % NX).wait_recv()

            @pl.when(gx + t < NX)
            def _():
                edge(1, t, g, (gx + t) % NX).wait_recv()

    def enter(r, _):
        rows = rows8(r)
        zero = jnp.zeros((8, 128), F32)

        def forward(n, state):
            a, b = state
            ra, rb = rcv[0, gx - n - 1, rows, 0:128], rcv[0, gx - n - 1, rows, 128:256]
            through = jnp.broadcast_to(ra[:, 0:1], (8, 128))
            return through * a + ra, through * b + rb

        a, b = lax.fori_loop(0, gx, forward, (zero, zero))
        ra, rb = pltpu.roll(a, 64, 1), pltpu.roll(b, 64, 1)
        inc[0, rows, 0:128] = jnp.where(low, ra, rb)
        inc[0, rows, 128:256] = jnp.where(low, rb, a)
        inc[0, rows, 256:384] = b

        def backward(n, state):
            a, b = state
            last = NX - 2 - gx - n
            ra, rb = rcv[1, last, rows, 0:128], rcv[1, last, rows, 128:256]
            through = jnp.broadcast_to(rb[:, 127:128], (8, 128))
            return through * a + ra, through * b + rb

        a, b = lax.fori_loop(0, NX - 1 - gx, backward, (zero, zero))
        ra, rb = pltpu.roll(a, 64, 1), pltpu.roll(b, 64, 1)
        inc[1, rows, 0:128] = a
        inc[1, rows, 128:256] = jnp.where(low, b, ra)
        inc[1, rows, 256:384] = jnp.where(low, ra, rb)
        return 0

    lax.fori_loop(0, 8, enter, 0)

    weights = wmat[...].astype(BF16)

    def moments(slot, dst, dst_row):
        for half in range(2):
            cols = pl.ds(pl.multiple_of(slot * 768 + half * 384, 128), 384)
            swept = val[:, :, cols] + reach[:, :, cols] * inc[...]
            val[:, :, cols] = swept
            flat = swept.reshape(128, 384)
            hi = flat.astype(BF16)
            lo = (flat - hi.astype(F32)).astype(BF16)
            both = jnp.dot(weights, jnp.concatenate([hi, lo], axis=0), preferred_element_type=F32)
            total = both[0:16] + both[16:32]
            for j in range(3):
                dst[pl.ds(pl.multiple_of(dst_row + (half * 3 + j) * 16, 16), 16), :] = total[:, j * 128 : (j + 1) * 128]

    def slot_rows(n):
        return pl.ds(pl.multiple_of(n * SLOT_ROWS, SLOT_ROWS), SLOT_ROWS)

    partner = vert_of(y, z, 1 - core)

    def to_core(n):
        return copy(stage.at[slot_rows(n), :], got_c.at[slot_rows(n), :], CR + n, CR + n, gx, partner)

    def other_half(n, _):
        moments((1 - core) * 4 + (y + n + 1) % NY, stage, n * SLOT_ROWS)
        to_core(n).start()
        return 0

    lax.fori_loop(0, 4, other_half, 0)

    def to_y(n):
        return copy(
            part.at[slot_rows(n), :], got_y.at[slot_rows(n), :], YR + n, YR + n, gx, vert_of((y + n + 1) % NY, z, core)
        )

    def own_half(n, _):
        moments(core * 4 + (y + n + 1) % NY, part, n * SLOT_ROWS)
        to_core(n).wait_recv()
        part[slot_rows(n), :] += got_c[slot_rows(n), :]

        @pl.when(n < 3)
        def _():
            to_y(n).start()

        return 0

    lax.fori_loop(0, 4, own_half, 0)
    for n in range(3):
        to_y(n).wait_recv()
        part[slot_rows(3), :] += got_y[slot_rows(n), :]

    def drain_sums():
        for n in range(4):
            to_core(n).wait_send()
        for n in range(3):
            to_y(n).wait_send()

    def tile_rows(n):
        return pl.ds(pl.multiple_of(n * 16, 16), 16)

    mine = core * 4 + y
    own_row = (1 + mine) * SLOT_ROWS

    def to_z(n):
        peer = (z + n + 1) % NZ
        return copy(
            part.at[pl.ds(pl.multiple_of(3 * SLOT_ROWS + peer * 16, 16), 16), :], got_z.at[tile_rows(n), :],
            ZR + n, ZR + n, gx, vert_of(y, peer, core),
        )

    def from_owner(n, owner, target):
        tile = pl.ds(pl.multiple_of(own_row + owner * 16, 16), 16)
        return copy(full.at[tile, :], full.at[tile, :], ZG + n, ZG + n, gx, vert_of(y, target, core))

    def drain_z():
        for n in range(7):
            @pl.when((z + n + 1) % NZ < SLOT)
            def _():
                to_z(n).wait_send()

    for n in range(7):
        @pl.when((z + n + 1) % NZ < SLOT)
        def _():
            to_z(n).start()

    @pl.when(z < SLOT)
    def _():
        total = part[pl.ds(pl.multiple_of(3 * SLOT_ROWS + z * 16, 16), 16), :]
        for n in range(7):
            copy(got_z.at[tile_rows(n), :], got_z.at[tile_rows(n), :], ZR + n, ZR + n, gx, vert).wait_recv()
            total += got_z[tile_rows(n), :]
        full[pl.ds(pl.multiple_of(own_row + z * 16, 16), 16), :] = total
        for n in range(7):
            from_owner(n, z, (z + n + 1) % NZ).start()

    for n in range(7):
        owner = (z + NZ - n - 1) % NZ

        @pl.when(owner < SLOT)
        def _():
            from_owner(n, owner, z).wait_recv()

    def slot_of(n):
        return pl.ds(pl.multiple_of((1 + n) * SLOT_ROWS, SLOT_ROWS), SLOT_ROWS)

    def gather_y(n, slot):
        return copy(
            full.at[slot_of(slot), :], full.at[slot_of(slot), :], YG + n, YG + n, gx, vert_of((y + n + 1) % NY, z, core)
        )

    halo_slot = jnp.where(core == 1, -1, 8)

    def send_halo(n):
        return copy(
            full.at[slot_of(mine), :], full.at[slot_of(halo_slot), :], HALO + n, HALO,
            jnp.where(core == 1, gx + 1, gx - 1), vert_of((y + n) % NY, z, core),
        )

    def gather_core(n, slot):
        return copy(full.at[slot_of(slot), :], full.at[slot_of(slot), :], CG + n, CG + n, gx, partner)

    for n in range(3):
        gather_y(n, mine).start()

    @pl.when(halo_source)
    def _():
        for n in range(4):
            send_halo(n).start()

    gather_core(3, mine).start()
    for n in range(3):
        slot = core * 4 + (y + NY - n - 1) % NY
        gather_y(n, slot).wait_recv()
        gather_core(n, slot).start()

    @pl.when(halo_here)
    def _():
        copy(full.at[slot_of(halo_slot), :], full.at[slot_of(halo_slot), :], HALO, HALO, gx, vert).wait_recv()
        gather_core(4, halo_slot).start()

    nothing = jnp.zeros((SLOT_ROWS, 128), F32)

    @pl.when(jnp.logical_not(has_left))
    def _():
        full[slot_of(-1), :] = nothing

    @pl.when(jnp.logical_not(has_right))
    def _():
        full[slot_of(8), :] = nothing

    for n in range(4):
        gather_core(n, (1 - core) * 4 + (y + NY - n - 1) % NY).wait_recv()

    other_halo = jnp.where(core == 1, 8, -1)

    @pl.when(jnp.where(core == 1, has_right, has_left))
    def _():
        gather_core(4, other_halo).wait_recv()

    for n in range(3):
        gather_y(n, mine).wait_send()

    @pl.when(halo_source)
    def _():
        for n in range(4):
            send_halo(n).wait_send()

    for n in range(4):
        gather_core(n, core * 4 + (y + NY - n - 1) % NY).wait_send()

    @pl.when(halo_here)
    def _():
        gather_core(4, halo_slot).wait_send()

    @pl.when(z < SLOT)
    def _():
        for n in range(7):
            from_owner(n, z, (z + n + 1) % NZ).wait_send()

    left_flag = jnp.where(has_left, 1.0, 0.0).astype(F32)
    right_flag = jnp.where(has_right, 1.0, 0.0).astype(F32)

    def smooth(src, dst, first, last, skip=0):
        def get(t):
            if t < 0 or t > 59:
                return [jnp.zeros((8, 128), F32)] * 2
            return [src[t * 16 + 8 * h : t * 16 + 8 * h + 8, :] for h in range(2)]

        def rolled(t):
            return [pltpu.roll(m, 64, 1) for m in get(t)]

        around = {t: rolled(t) for t in range(first - 2, first + 2)}
        for t in range(first, last + 1):
            around[t + 2] = rolled(t + 2)
            here = get(t)
            density = jnp.broadcast_to(here[0][0:1, :], (8, 128))
            coef = SMOOTH_RATE / (1.0 + density * density)
            if t < SLOT:
                coef = coef * left_flag
            if t >= 54:
                coef = coef * right_flag
            for h in range(2):
                before = jnp.where(low, around[t - 2][h], around[t - 1][h])
                after = jnp.where(low, around[t + 1][h], around[t + 2][h])
                dst[(t - skip) * 16 + 8 * h : (t - skip) * 16 + 8 * h + 8, :] = here[h] + coef * (before + after - 2.0 * here[h])
            del around[t - 2]

    smooth(full, tmp, 1, 58)
    smooth(tmp, full, 3, 56)
    smooth(full, tmp, 4, 55)
    smooth(tmp, moved, 6, 53, 6)
    drain_x()
    drain_sums()
    drain_z()


def relax_kernel(val, moved, phit, out, mac, mac_buf, coef_f, coef_l, keep, buf, out_sem, mac_sem):
    for t in range(TILES):
        mac_buf[:, t * 128 : (t + 1) * 128] = moved[t * 16 : t * 16 + 13, :]
    mac_copy = pltpu.make_async_copy(mac_buf, mac, mac_sem)
    mac_copy.start()

    def row(k):
        return jnp.tanh(moved[pl.ds(k, TILES, stride=16), :])

    density = 1.0 + 0.5 * row(0)
    ux, uy, uz = 0.5 * row(1), 0.5 * row(2), 0.5 * row(3)
    g = 1.0 / (1.0 + 0.5 * row(4))
    s0, s1, s2, s3, s4 = [0.2 * row(5 + j) for j in range(5)]
    qx, qy, qz = [0.2 * row(10 + j) for j in range(3)]
    front = density * g * jnp.sqrt(g)
    h = 0.5 * g
    sxx, syy = 0.5 * s3, 0.5 * s4
    szz = -(sxx + syy)
    square = ux * ux + uy * uy + uz * uz
    a = qx * ux + qy * uy + qz * uz
    b = h * square - 2.5
    ah = a * h
    scale = front * g
    quad = (
        ux * (sxx * ux + s0 * uy + s1 * uz) + uy * (syy * uy + s2 * uz) + szz * uz * uz
    )
    values_f = [
        scale * h * qx, scale * h * qy, scale * h * qz,
        scale * (sxx - g * qx * ux - ah),
        scale * (syy - g * qy * uy - ah),
        scale * (szz - g * qz * uz - ah),
        scale * (s0 - g * (qx * uy + qy * ux)),
        scale * (s1 - g * (qx * uz + qz * ux)),
        scale * (s2 - g * (qy * uz + qz * uy)),
        scale * (b * qx + 2.0 * ah * ux - (2.0 * sxx * ux + s0 * uy + s1 * uz)),
        scale * (b * qy + 2.0 * ah * uy - (s0 * ux + 2.0 * syy * uy + s2 * uz)),
        scale * (b * qz + 2.0 * ah * uz - (s1 * ux + s2 * uy + 2.0 * szz * uz)),
        front + scale * (quad - a * b),
    ]
    le = -LOG2E * h
    none = jnp.zeros_like(le)
    values_l = [none] * 3 + [le] * 3 + [none] * 3 + [-2.0 * le * ux, -2.0 * le * uy, -2.0 * le * uz, le * square]
    for n in range(16):
        coef_f[pl.ds(n, TILES, stride=16), :] = values_f[n] if n < 13 else none
        coef_l[pl.ds(n, TILES, stride=16), :] = values_l[n] if n < 13 else none

    lhs_f = phit[:, 0:48].astype(BF16)
    lhs_l = phit[:, 48:96].astype(BF16)
    keep[...] = jnp.broadcast_to(phit[:, 96:97], (128, 128))

    def split(ref, n):
        c = jnp.concatenate([ref[pl.ds(pl.multiple_of(n * 48 + 16 * j, 16), 16), :] for j in range(3)], axis=1)
        hi = c.astype(BF16)
        lo = (c - hi.astype(F32)).astype(BF16)
        return jnp.concatenate([hi, lo, hi], axis=0)

    def put(n):
        cols = pl.ds(pl.multiple_of(n * 384, 128), 384)
        return pltpu.make_async_copy(buf.at[n % BUFS], out.at[:, :, cols], out_sem.at[n % BUFS])

    def relaxed(n, _):
        @pl.when(n >= BUFS)
        def _():
            put(n - BUFS).wait()

        poly = jnp.dot(lhs_f, split(coef_f, n), preferred_element_type=F32)
        power = jnp.dot(lhs_l, split(coef_l, n), preferred_element_type=F32)
        for j in range(3):
            cols = pl.ds(pl.multiple_of(n * 384 + j * 128, 128), 128)
            part = slice(j * 128, (j + 1) * 128)
            swept = val[:, :, cols].reshape(128, 128)
            buf[n % BUFS, :, :, part] = (keep[...] * swept + poly[:, part] * jnp.exp2(power[:, part])).reshape(2, 64, 128)
        put(n).start()
        return 0

    lax.fori_loop(0, 16, relaxed, 0)
    for n in range(16 - BUFS, 16):
        put(n).wait()
    mac_copy.wait()


def per_device(dist, factors, velocity, weights, relax):
    vmem = pl.BlockSpec(memory_space=pltpu.VMEM)
    hbm = pl.BlockSpec(memory_space=pltpu.HBM)
    operands = (dist, jnp.transpose(factors, (0, 2, 1)), velocity, weights, relax)
    swept, moved, phit = pl.pallas_call(
        kernel,
        out_shape=(
            jax.ShapeDtypeStruct((2, 64, 6144), F32),
            jax.ShapeDtypeStruct((TILES * 16, 128), F32),
            jax.ShapeDtypeStruct((128, 128), F32),
        ),
        in_specs=[hbm] * 5,
        out_specs=(vmem, vmem, vmem),
        scratch_shapes=[
            pltpu.VMEM((2, 32, 64), F32),
            pltpu.VMEM((3, 2, 64), F32),
            pltpu.VMEM((13, 2, 64), F32),
            pltpu.VMEM((2, 64), F32),
            pltpu.VMEM((256, 128), BF16),
            pltpu.VMEM((2, 64, 6144), F32),
            pltpu.VMEM((2, 64, 6144), F32),
            pltpu.VMEM((2, 64, 256), F32),
            pltpu.VMEM((2, 3, 64, 256), F32),
            pltpu.VMEM((2, 64, 384), F32),
            pltpu.VMEM((32, 256), F32),
            pltpu.VMEM((128, 128), F32),
            pltpu.VMEM((4 * SLOT_ROWS, 128), F32),
            pltpu.VMEM((4 * SLOT_ROWS, 128), F32),
            pltpu.VMEM((4 * SLOT_ROWS, 128), F32),
            pltpu.VMEM((3 * SLOT_ROWS, 128), F32),
            pltpu.VMEM((7 * 16, 128), F32),
            pltpu.VMEM((10 * SLOT_ROWS, 128), F32),
            pltpu.VMEM((10 * SLOT_ROWS, 128), F32),
            pltpu.SemaphoreType.DMA((8,)),
            pltpu.SemaphoreType.DMA((4,)),
            pltpu.SemaphoreType.DMA((N_SEM,)),
            pltpu.SemaphoreType.DMA((N_SEM,)),
        ],
        compiler_params=pltpu.CompilerParams(
            collective_id=0, has_side_effects=True, vmem_limit_bytes=40 * 2**20
        ),
    )(*[pltpu.with_memory_space_constraint(x, pltpu.HBM) for x in operands])
    return pl.pallas_call(
        relax_kernel,
        out_shape=(
            jax.ShapeDtypeStruct((2, 64, 6144), F32),
            jax.ShapeDtypeStruct((13, 6144), F32),
        ),
        in_specs=[vmem] * 3,
        out_specs=(hbm, hbm),
        scratch_shapes=[
            pltpu.VMEM((13, 6144), F32),
            pltpu.VMEM((TILES * 16, 128), F32),
            pltpu.VMEM((TILES * 16, 128), F32),
            pltpu.VMEM((128, 128), F32),
            pltpu.VMEM((BUFS, 2, 64, 384), F32),
            pltpu.SemaphoreType.DMA((BUFS,)),
            pltpu.SemaphoreType.DMA,
        ],
        compiler_params=pltpu.CompilerParams(vmem_limit_bytes=32 * 2**20),
    )(swept, moved, phit)


def solution(mesh):
    return jax.shard_map(
        per_device,
        mesh=mesh,
        in_specs=(
            P(None, "vert", "gx"),
            P(None, "vert", "gx"),
            P(None, None, "vert"),
            P(None, None, "vert"),
            P(None, "vert"),
        ),
        out_specs=(P(None, "vert", "gx"), P(None, "gx")),
        check_vma=False,
    )
```

```python
import functools

import jax
import jax.numpy as jnp
from jax import lax
from jax.experimental import pallas as pl
from jax.experimental.pallas import tpu as pltpu
from jax.sharding import PartitionSpec as P

MESH = pl.DeviceIdType.MESH
F32, BF16 = jnp.float32, jnp.bfloat16
SMOOTH_RATE = 0.24
LOG2E = 1.4426950408889634

NX, NY, NZ = 4, 4, 8
TILES, SLOT = 48, 6
SLOT_ROWS = SLOT * 16
GROUPS = 2
BUFS = 4

XF, CR = 0, 6 * GROUPS
YR = CR + 4
ZR = YR + 3
ZG = ZR + 7
YG = ZG + 7
CG = YG + 3
HALO = CG + 5
N_SEM = HALO + 4


def kernel(
    dist, fac_hbm, vel_hbm, wgt_hbm, rel_hbm, val, moved, phit,
    fac, vel, wgt, rel, lhs, reach, scaled, spread_f, snd, rcv, inc, wmat, phi,
    stage, part, got_c, got_y, got_z, full, tmp, ld_sem, small_sem, ssem, rsem,
):
    gx = lax.axis_index("gx")
    vert = lax.axis_index("vert")
    y = vert // 16
    z = (vert // 2) % 8
    core = vert % 2

    def vert_of(y_, z_, core_):
        return y_ * 16 + z_ * 2 + core_

    def copy(src, dst, send, recv, x_, v_):
        return pltpu.make_async_remote_copy(
            src_ref=src, dst_ref=dst, send_sem=ssem.at[send], recv_sem=rsem.at[recv],
            device_id=(x_, v_), device_id_type=MESH,
        )

    def rows8(r):
        return pl.ds(pl.multiple_of(r * 8, 8), 8)

    def load(r):
        return pltpu.make_async_copy(dist.at[:, rows8(r), :], val.at[:, rows8(r), :], ld_sem.at[r])

    small = [
        pltpu.make_async_copy(src, dst, small_sem.at[n])
        for n, (src, dst) in enumerate(((fac_hbm, fac), (wgt_hbm, wgt), (vel_hbm, vel), (rel_hbm, rel)))
    ]
    for one_copy in small:
        one_copy.start()
    for r in range(8):
        load(r).start()

    barrier = pltpu.get_barrier_semaphore()

    def greet(x_, v_):
        pl.semaphore_signal(barrier, inc=1, device_id=(x_, v_), device_id_type=MESH)

    for t in range(1, NX):
        greet((gx + t) % NX, vert)
    greet(gx, vert_of(y, z, 1 - core))
    for t in range(1, NY):
        greet(gx, vert_of((y + t) % NY, z, core))
    for t in range(1, NZ):
        greet(gx, vert_of(y, (z + t) % NZ, core))
    has_left, has_right = gx > 0, gx < NX - 1
    halo_here = jnp.where(core == 1, has_left, has_right)
    halo_x = jnp.where(core == 1, gx - 1, gx + 1)
    halo_y = jnp.where(core == 1, NY - 1, 0)

    @pl.when(halo_here & (y != halo_y))
    def _():
        greet(halo_x, vert_of(halo_y, z, core))

    halo_source = ((core == 1) & (y == NY - 1) & has_right) | ((core == 0) & (y == 0) & has_left)

    lane = lax.broadcasted_iota(jnp.int32, (8, 128), 1)
    low = lane < 64

    def lanes2(a, b):
        return jnp.concatenate([a, b], axis=1)

    small[0].wait()
    f = lanes2(fac[0], fac[1])
    q = jnp.sqrt(1.0 - f * f)
    at = lax.broadcasted_iota(jnp.int32, (32, 128), 0)
    ahead = lax.broadcasted_iota(jnp.int32, (32, 128), 1) < 64

    def down(x, k):
        return jnp.where(at >= k, pltpu.roll(x, k, 0), 1.0)

    def up(x, k):
        return jnp.where(at < 32 - k, pltpu.roll(x, 32 - k, 0), 1.0)

    before, after = f, f
    for k in (1, 2, 4, 8, 16):
        before, after = before * down(before, k), after * up(after, k)
    to_edge = q * jnp.where(ahead, up(after, 1), down(before, 1))

    def exact(x, n, extra):
        hi = x.astype(BF16).astype(F32)
        mid = (x - hi).astype(BF16).astype(F32)
        turned = jnp.concatenate([hi, mid, x - hi - mid, extra], axis=0).T
        lhs[n * 128 : (n + 1) * 128, :] = turned.astype(BF16)
        return turned

    def picks(p):
        cell = lax.broadcasted_iota(jnp.int32, (96, 384), 0) % 32
        second = lax.broadcasted_iota(jnp.int32, (96, 384), 1) >= 192
        return jnp.where(cell == 2 * p + jnp.where(second, 1, 0), 1.0, 0.0).astype(BF16)

    def spread(first, refs, unroll):
        def some(n, _):
            for k in range(unroll):
                p = n * unroll + k
                cols = pl.ds(pl.multiple_of(p * 384, 128), 384)
                rows = lhs[first * 128 : (first + len(refs)) * 128, 0:96]
                wide = jnp.dot(rows, picks(p), preferred_element_type=F32)
                for m, ref in enumerate(refs):
                    ref[:, :, cols] = wide[m * 128 : (m + 1) * 128].reshape(2, 64, 384)
            return 0

        lax.fori_loop(0, 16 // unroll, some, 0)

    phi[...] = exact(to_edge, 0, after)
    spread(0, [scaled], 4)

    def leave(r):
        rows = rows8(r)
        for d in range(2):
            total = [None] * 3
            for t in range(TILES):
                term = scaled[d, rows, t * 128 : (t + 1) * 128] * val[d, rows, t * 128 : (t + 1) * 128]
                total[t % 3] = term if total[t % 3] is None else total[t % 3] + term
            a, b, c = total
            through = jnp.broadcast_to(phi[pl.ds(pl.multiple_of(d * 64 + r * 8, 8), 8), 96:97], (8, 128))
            if d == 0:
                ra, rb = pltpu.roll(a, 64, 1), pltpu.roll(b, 64, 1)
                snd[0, rows, 0:128] = jnp.where(low, through, b + ra)
                snd[0, rows, 128:256] = c + jnp.where(low, ra, rb)
            else:
                rb, rc = pltpu.roll(b, 64, 1), pltpu.roll(c, 64, 1)
                snd[1, rows, 0:128] = a + jnp.where(low, rb, rc)
                snd[1, rows, 128:256] = jnp.where(low, b + rc, through)

    def edge(direction, t, g, target):
        span = pl.ds(g * (64 // GROUPS), 64 // GROUPS)
        n = XF + (direction * 3 + t - 1) * GROUPS + g
        return copy(snd.at[direction, span, :], rcv.at[direction, t - 1, span, :], n, n, target, vert)

    def drain_x():
        for g in range(GROUPS):
            for t in range(1, NX):
                @pl.when(gx + t < NX)
                def _():
                    edge(0, t, g, (gx + t) % NX).wait_send()

                @pl.when(gx - t >= 0)
                def _():
                    edge(1, t, g, (gx - t) % NX).wait_send()

    for g in range(GROUPS):
        def leave_rows(r, _):
            load(r).wait()
            leave(r)
            return 0

        lax.fori_loop(g * 8 // GROUPS, (g + 1) * 8 // GROUPS, leave_rows, 0)
        if g == 0:
            pl.semaphore_wait(barrier, 14 + jnp.where(halo_source, 3, 0))

        for t in (2, 1, 3):
            @pl.when(gx + t < NX)
            def _():
                edge(0, t, g, gx + t).start()

            @pl.when(gx - t >= 0)
            def _():
                edge(1, t, g, gx - t).start()

    for one_copy in small[1:]:
        one_copy.wait()
    wmat[...] = jnp.zeros_like(wmat)
    for k in range(13):
        row = lanes2(wgt[k, 0:1, :], wgt[k, 1:2, :])
        hi = row.astype(BF16).astype(F32)
        lo = row - hi
        wmat[k : k + 1, 0:128] = hi
        wmat[k : k + 1, 128:256] = hi
        wmat[16 + k : 17 + k, 0:128] = lo

    vx, vy, vz = [lanes2(vel[j, 0:1, :], vel[j, 1:2, :]) for j in range(3)]
    relax = lanes2(rel[0:1, :], rel[1:2, :])
    xx, yy, zz = vx * vx, vy * vy, vz * vz
    sq = xx + yy + zz
    one = jnp.ones_like(vx)
    feats = [vx * sq, vy * sq, vz * sq, xx, yy, zz, vx * vy, vx * vz, vy * vz, vx, vy, vz, one]
    phi[...] = jnp.zeros_like(phi)
    for n, feat in enumerate(feats):
        for base, term in ((0, feat * relax), (48, feat)):
            hi = term.astype(BF16).astype(F32)
            phi[base + n : base + n + 1, :] = hi
            phi[base + 16 + n : base + 17 + n, :] = hi
            phi[base + 32 + n : base + 33 + n, :] = term - hi
    phi[96:97, :] = 1.0 - relax
    phit[...] = phi[...].T

    exact(f, 1, f)
    exact(q, 2, q)
    exact(jnp.where(ahead, before, after), 3, f)
    spread(1, [spread_f, scaled, reach], 2)

    def sweep(r):
        rows = rows8(r)
        zero = jnp.zeros((8, 128), F32)
        ones = jnp.ones((8, 128), F32)

        def cols(t):
            return pl.ds(t * 128, 128)

        value = [[zero] * 3, [zero] * 3]
        rolls = [[zero, zero], [zero, zero]]
        f_near = [ones, ones]
        for step in range(16):
            for d in range(2):
                p = step if d == 0 else 15 - step
                f = [spread_f[d, rows, cols(3 * p + j)] for j in range(3)]
                first, second = (f[0], f[2]) if d == 0 else (f[2], f[0])
                near, far = first * f_near[d], second * first
                f_near[d] = second
                if d == 0:
                    gs = [near, jnp.where(low, near, far), far]
                else:
                    gs = [far, jnp.where(low, far, near), near]
                for j in (0, 1, 2) if d == 0 else (2, 1, 0):
                    t = 3 * p + j
                    s = scaled[d, rows, cols(t)] * val[d, rows, cols(t)]
                    two_off, one_off = rolls[d]
                    neighbour = jnp.where(low, two_off, one_off) if d == 0 else jnp.where(low, one_off, two_off)
                    rolls[d] = [one_off, pltpu.roll(s, 64, 1)]
                    value[d][j] = gs[j] * value[d][j] + (s + f[j] * neighbour)
                    val[d, rows, cols(t)] = value[d][j]

    def sweep_rows(r, _):
        sweep(r)
        return 0

    lax.fori_loop(0, 8, sweep_rows, 0)

    for t in range(1, NX):
        for g in range(GROUPS):
            @pl.when(gx - t >= 0)
            def _():
                edge(0, t, g, (gx - t) % NX).wait_recv()

            @pl.when(gx + t < NX)
            def _():
                edge(1, t, g, (gx + t) % NX).wait_recv()

    def enter(r, _):
        rows = rows8(r)
        zero = jnp.zeros((8, 128), F32)

        def forward(n, state):
            a, b = state
            ra, rb = rcv[0, gx - n - 1, rows, 0:128], rcv[0, gx - n - 1, rows, 128:256]
            through = jnp.broadcast_to(ra[:, 0:1], (8, 128))
            return through * a + ra, through * b + rb

        a, b = lax.fori_loop(0, gx, forward, (zero, zero))
        ra, rb = pltpu.roll(a, 64, 1), pltpu.roll(b, 64, 1)
        inc[0, rows, 0:128] = jnp.where(low, ra, rb)
        inc[0, rows, 128:256] = jnp.where(low, rb, a)
        inc[0, rows, 256:384] = b

        def backward(n, state):
            a, b = state
            last = NX - 2 - gx - n
            ra, rb = rcv[1, last, rows, 0:128], rcv[1, last, rows, 128:256]
            through = jnp.broadcast_to(rb[:, 127:128], (8, 128))
            return through * a + ra, through * b + rb

        a, b = lax.fori_loop(0, NX - 1 - gx, backward, (zero, zero))
        ra, rb = pltpu.roll(a, 64, 1), pltpu.roll(b, 64, 1)
        inc[1, rows, 0:128] = a
        inc[1, rows, 128:256] = jnp.where(low, b, ra)
        inc[1, rows, 256:384] = jnp.where(low, ra, rb)
        return 0

    lax.fori_loop(0, 8, enter, 0)

    weights = wmat[...].astype(BF16)

    def moments(slot, dst, dst_row):
        for half in range(2):
            cols = pl.ds(pl.multiple_of(slot * 768 + half * 384, 128), 384)
            swept = val[:, :, cols] + reach[:, :, cols] * inc[...]
            val[:, :, cols] = swept
            flat = swept.reshape(128, 384)
            hi = flat.astype(BF16)
            lo = (flat - hi.astype(F32)).astype(BF16)
            both = jnp.dot(weights, jnp.concatenate([hi, lo], axis=0), preferred_element_type=F32)
            total = both[0:16] + both[16:32]
            for j in range(3):
                dst[pl.ds(pl.multiple_of(dst_row + (half * 3 + j) * 16, 16), 16), :] = total[:, j * 128 : (j + 1) * 128]

    def slot_rows(n):
        return pl.ds(pl.multiple_of(n * SLOT_ROWS, SLOT_ROWS), SLOT_ROWS)

    partner = vert_of(y, z, 1 - core)

    def to_core(n):
        return copy(stage.at[slot_rows(n), :], got_c.at[slot_rows(n), :], CR + n, CR + n, gx, partner)

    def other_half(n, _):
        moments((1 - core) * 4 + (y + n + 1) % NY, stage, n * SLOT_ROWS)
        to_core(n).start()
        return 0

    lax.fori_loop(0, 4, other_half, 0)

    def to_y(n):
        return copy(
            part.at[slot_rows(n), :], got_y.at[slot_rows(n), :], YR + n, YR + n, gx, vert_of((y + n + 1) % NY, z, core)
        )

    def own_half(n, _):
        moments(core * 4 + (y + n + 1) % NY, part, n * SLOT_ROWS)
        to_core(n).wait_recv()
        part[slot_rows(n), :] += got_c[slot_rows(n), :]

        @pl.when(n < 3)
        def _():
            to_y(n).start()

        return 0

    lax.fori_loop(0, 4, own_half, 0)
    for n in range(3):
        to_y(n).wait_recv()
        part[slot_rows(3), :] += got_y[slot_rows(n), :]

    def drain_sums():
        for n in range(4):
            to_core(n).wait_send()
        for n in range(3):
            to_y(n).wait_send()

    def tile_rows(n):
        return pl.ds(pl.multiple_of(n * 16, 16), 16)

    mine = core * 4 + y
    own_row = (1 + mine) * SLOT_ROWS

    def to_z(n):
        peer = (z + n + 1) % NZ
        return copy(
            part.at[pl.ds(pl.multiple_of(3 * SLOT_ROWS + peer * 16, 16), 16), :], got_z.at[tile_rows(n), :],
            ZR + n, ZR + n, gx, vert_of(y, peer, core),
        )

    def from_owner(n, owner, target):
        tile = pl.ds(pl.multiple_of(own_row + owner * 16, 16), 16)
        return copy(full.at[tile, :], full.at[tile, :], ZG + n, ZG + n, gx, vert_of(y, target, core))

    def drain_z():
        for n in range(7):
            @pl.when((z + n + 1) % NZ < SLOT)
            def _():
                to_z(n).wait_send()

    far_first = (3, 2, 4, 1, 5, 0, 6)
    for n in far_first:
        @pl.when((z + n + 1) % NZ < SLOT)
        def _():
            to_z(n).start()

    @pl.when(z < SLOT)
    def _():
        total = part[pl.ds(pl.multiple_of(3 * SLOT_ROWS + z * 16, 16), 16), :]
        for n in range(7):
            copy(got_z.at[tile_rows(n), :], got_z.at[tile_rows(n), :], ZR + n, ZR + n, gx, vert).wait_recv()
            total += got_z[tile_rows(n), :]
        full[pl.ds(pl.multiple_of(own_row + z * 16, 16), 16), :] = total
        for n in far_first:
            from_owner(n, z, (z + n + 1) % NZ).start()

    for n in range(7):
        owner = (z + NZ - n - 1) % NZ

        @pl.when(owner < SLOT)
        def _():
            from_owner(n, owner, z).wait_recv()

    def slot_of(n):
        return pl.ds(pl.multiple_of((1 + n) * SLOT_ROWS, SLOT_ROWS), SLOT_ROWS)

    def gather_y(n, slot):
        return copy(
            full.at[slot_of(slot), :], full.at[slot_of(slot), :], YG + n, YG + n, gx, vert_of((y + n + 1) % NY, z, core)
        )

    halo_slot = jnp.where(core == 1, -1, 8)

    def send_halo(n):
        return copy(
            full.at[slot_of(mine), :], full.at[slot_of(halo_slot), :], HALO + n, HALO,
            jnp.where(core == 1, gx + 1, gx - 1), vert_of((y + n) % NY, z, core),
        )

    def gather_core(n, slot):
        return copy(full.at[slot_of(slot), :], full.at[slot_of(slot), :], CG + n, CG + n, gx, partner)

    @pl.when(halo_source)
    def _():
        for n in (2, 1, 3, 0):
            send_halo(n).start()

    for n in (1, 0, 2):
        gather_y(n, mine).start()

    gather_core(3, mine).start()
    for n in (0, 2, 1):
        slot = core * 4 + (y + NY - n - 1) % NY
        gather_y(n, slot).wait_recv()
        gather_core(n, slot).start()

    @pl.when(halo_here)
    def _():
        copy(full.at[slot_of(halo_slot), :], full.at[slot_of(halo_slot), :], HALO, HALO, gx, vert).wait_recv()
        gather_core(4, halo_slot).start()

    nothing = jnp.zeros((SLOT_ROWS, 128), F32)

    @pl.when(jnp.logical_not(has_left))
    def _():
        full[slot_of(-1), :] = nothing

    @pl.when(jnp.logical_not(has_right))
    def _():
        full[slot_of(8), :] = nothing

    for n in range(4):
        gather_core(n, (1 - core) * 4 + (y + NY - n - 1) % NY).wait_recv()

    other_halo = jnp.where(core == 1, 8, -1)

    @pl.when(jnp.where(core == 1, has_right, has_left))
    def _():
        gather_core(4, other_halo).wait_recv()

    for n in range(3):
        gather_y(n, mine).wait_send()

    @pl.when(halo_source)
    def _():
        for n in range(4):
            send_halo(n).wait_send()

    for n in range(4):
        gather_core(n, core * 4 + (y + NY - n - 1) % NY).wait_send()

    @pl.when(halo_here)
    def _():
        gather_core(4, halo_slot).wait_send()

    @pl.when(z < SLOT)
    def _():
        for n in range(7):
            from_owner(n, z, (z + n + 1) % NZ).wait_send()

    left_flag = jnp.where(has_left, 1.0, 0.0).astype(F32)
    right_flag = jnp.where(has_right, 1.0, 0.0).astype(F32)

    def smooth(src, dst, first, last, skip=0):
        def get(t):
            if t < 0 or t > 59:
                return [jnp.zeros((8, 128), F32)] * 2
            return [src[t * 16 + 8 * h : t * 16 + 8 * h + 8, :] for h in range(2)]

        def rolled(t):
            return [pltpu.roll(m, 64, 1) for m in get(t)]

        around = {t: rolled(t) for t in range(first - 2, first + 2)}
        for t in range(first, last + 1):
            around[t + 2] = rolled(t + 2)
            here = get(t)
            density = jnp.broadcast_to(here[0][0:1, :], (8, 128))
            coef = SMOOTH_RATE / (1.0 + density * density)
            if t < SLOT:
                coef = coef * left_flag
            if t >= 54:
                coef = coef * right_flag
            for h in range(2):
                before = jnp.where(low, around[t - 2][h], around[t - 1][h])
                after = jnp.where(low, around[t + 1][h], around[t + 2][h])
                dst[(t - skip) * 16 + 8 * h : (t - skip) * 16 + 8 * h + 8, :] = here[h] + coef * (before + after - 2.0 * here[h])
            del around[t - 2]

    smooth(full, tmp, 1, 58)
    smooth(tmp, full, 3, 56)
    smooth(full, tmp, 4, 55)
    smooth(tmp, moved, 6, 53, 6)
    drain_x()
    drain_sums()
    drain_z()


def relax_kernel(val, moved, phit, out, mac, mac_buf, coef_f, coef_l, keep, buf, out_sem, mac_sem):
    for t in range(TILES):
        mac_buf[:, t * 128 : (t + 1) * 128] = moved[t * 16 : t * 16 + 13, :]
    mac_copy = pltpu.make_async_copy(mac_buf, mac, mac_sem)
    mac_copy.start()

    def row(k):
        return jnp.tanh(moved[pl.ds(k, TILES, stride=16), :])

    density = 1.0 + 0.5 * row(0)
    ux, uy, uz = 0.5 * row(1), 0.5 * row(2), 0.5 * row(3)
    g = 1.0 / (1.0 + 0.5 * row(4))
    s0, s1, s2, s3, s4 = [0.2 * row(5 + j) for j in range(5)]
    qx, qy, qz = [0.2 * row(10 + j) for j in range(3)]
    front = density * g * jnp.sqrt(g)
    h = 0.5 * g
    sxx, syy = 0.5 * s3, 0.5 * s4
    szz = -(sxx + syy)
    square = ux * ux + uy * uy + uz * uz
    a = qx * ux + qy * uy + qz * uz
    b = h * square - 2.5
    ah = a * h
    scale = front * g
    quad = (
        ux * (sxx * ux + s0 * uy + s1 * uz) + uy * (syy * uy + s2 * uz) + szz * uz * uz
    )
    values_f = [
        scale * h * qx, scale * h * qy, scale * h * qz,
        scale * (sxx - g * qx * ux - ah),
        scale * (syy - g * qy * uy - ah),
        scale * (szz - g * qz * uz - ah),
        scale * (s0 - g * (qx * uy + qy * ux)),
        scale * (s1 - g * (qx * uz + qz * ux)),
        scale * (s2 - g * (qy * uz + qz * uy)),
        scale * (b * qx + 2.0 * ah * ux - (2.0 * sxx * ux + s0 * uy + s1 * uz)),
        scale * (b * qy + 2.0 * ah * uy - (s0 * ux + 2.0 * syy * uy + s2 * uz)),
        scale * (b * qz + 2.0 * ah * uz - (s1 * ux + s2 * uy + 2.0 * szz * uz)),
        front + scale * (quad - a * b),
    ]
    le = -LOG2E * h
    none = jnp.zeros_like(le)
    values_l = [none] * 3 + [le] * 3 + [none] * 3 + [-2.0 * le * ux, -2.0 * le * uy, -2.0 * le * uz, le * square]
    for n in range(16):
        coef_f[pl.ds(n, TILES, stride=16), :] = values_f[n] if n < 13 else none
        coef_l[pl.ds(n, TILES, stride=16), :] = values_l[n] if n < 13 else none

    lhs_f = phit[:, 0:48].astype(BF16)
    lhs_l = phit[:, 48:96].astype(BF16)
    keep[...] = jnp.broadcast_to(phit[:, 96:97], (128, 128))

    def split(ref, n):
        c = jnp.concatenate([ref[pl.ds(pl.multiple_of(n * 48 + 16 * j, 16), 16), :] for j in range(3)], axis=1)
        hi = c.astype(BF16)
        lo = (c - hi.astype(F32)).astype(BF16)
        return jnp.concatenate([hi, lo, hi], axis=0)

    def put(n):
        cols = pl.ds(pl.multiple_of(n * 384, 128), 384)
        return pltpu.make_async_copy(buf.at[n % BUFS], out.at[:, :, cols], out_sem.at[n % BUFS])

    def relaxed(n, _):
        @pl.when(n >= BUFS)
        def _():
            put(n - BUFS).wait()

        poly = jnp.dot(lhs_f, split(coef_f, n), preferred_element_type=F32)
        power = jnp.dot(lhs_l, split(coef_l, n), preferred_element_type=F32)
        for j in range(3):
            cols = pl.ds(pl.multiple_of(n * 384 + j * 128, 128), 128)
            part = slice(j * 128, (j + 1) * 128)
            swept = val[:, :, cols].reshape(128, 128)
            buf[n % BUFS, :, :, part] = (keep[...] * swept + poly[:, part] * jnp.exp2(power[:, part])).reshape(2, 64, 128)
        put(n).start()
        return 0

    def two(n, _):
        relaxed(2 * n, 0)
        relaxed(2 * n + 1, 0)
        return 0

    lax.fori_loop(0, 8, two, 0)
    for n in range(16 - BUFS, 16):
        put(n).wait()
    mac_copy.wait()


def per_device(dist, factors, velocity, weights, relax):
    vmem = pl.BlockSpec(memory_space=pltpu.VMEM)
    hbm = pl.BlockSpec(memory_space=pltpu.HBM)
    operands = (dist, jnp.transpose(factors, (0, 2, 1)), velocity, weights, relax)
    swept, moved, phit = pl.pallas_call(
        kernel,
        out_shape=(
            jax.ShapeDtypeStruct((2, 64, 6144), F32),
            jax.ShapeDtypeStruct((TILES * 16, 128), F32),
            jax.ShapeDtypeStruct((128, 128), F32),
        ),
        in_specs=[hbm] * 5,
        out_specs=(vmem, vmem, vmem),
        scratch_shapes=[
            pltpu.VMEM((2, 32, 64), F32),
            pltpu.VMEM((3, 2, 64), F32),
            pltpu.VMEM((13, 2, 64), F32),
            pltpu.VMEM((2, 64), F32),
            pltpu.VMEM((512, 128), BF16),
            pltpu.VMEM((2, 64, 6144), F32),
            pltpu.VMEM((2, 64, 6144), F32),
            pltpu.VMEM((2, 64, 6144), F32),
            pltpu.VMEM((2, 64, 256), F32),
            pltpu.VMEM((2, 3, 64, 256), F32),
            pltpu.VMEM((2, 64, 384), F32),
            pltpu.VMEM((32, 256), F32),
            pltpu.VMEM((128, 128), F32),
            pltpu.VMEM((4 * SLOT_ROWS, 128), F32),
            pltpu.VMEM((4 * SLOT_ROWS, 128), F32),
            pltpu.VMEM((4 * SLOT_ROWS, 128), F32),
            pltpu.VMEM((3 * SLOT_ROWS, 128), F32),
            pltpu.VMEM((7 * 16, 128), F32),
            pltpu.VMEM((10 * SLOT_ROWS, 128), F32),
            pltpu.VMEM((10 * SLOT_ROWS, 128), F32),
            pltpu.SemaphoreType.DMA((8,)),
            pltpu.SemaphoreType.DMA((4,)),
            pltpu.SemaphoreType.DMA((N_SEM,)),
            pltpu.SemaphoreType.DMA((N_SEM,)),
        ],
        compiler_params=pltpu.CompilerParams(
            collective_id=0, has_side_effects=True, vmem_limit_bytes=40 * 2**20
        ),
    )(*[pltpu.with_memory_space_constraint(x, pltpu.HBM) for x in operands])
    return pl.pallas_call(
        relax_kernel,
        out_shape=(
            jax.ShapeDtypeStruct((2, 64, 6144), F32),
            jax.ShapeDtypeStruct((13, 6144), F32),
        ),
        in_specs=[vmem] * 3,
        out_specs=(hbm, hbm),
        scratch_shapes=[
            pltpu.VMEM((13, 6144), F32),
            pltpu.VMEM((TILES * 16, 128), F32),
            pltpu.VMEM((TILES * 16, 128), F32),
            pltpu.VMEM((128, 128), F32),
            pltpu.VMEM((BUFS, 2, 64, 384), F32),
            pltpu.SemaphoreType.DMA((BUFS,)),
            pltpu.SemaphoreType.DMA,
        ],
        compiler_params=pltpu.CompilerParams(vmem_limit_bytes=32 * 2**20),
    )(swept, moved, phit)


def solution(mesh):
    return jax.shard_map(
        per_device,
        mesh=mesh,
        in_specs=(
            P(None, "vert", "gx"),
            P(None, "vert", "gx"),
            P(None, None, "vert"),
            P(None, None, "vert"),
            P(None, "vert"),
        ),
        out_specs=(P(None, "vert", "gx"), P(None, "gx")),
        check_vma=False,
    )
```

```python
import functools

import jax
import jax.numpy as jnp
from jax import lax
from jax.experimental import pallas as pl
from jax.experimental.pallas import tpu as pltpu
from jax.sharding import PartitionSpec as P

MESH = pl.DeviceIdType.MESH
F32, BF16 = jnp.float32, jnp.bfloat16
SMOOTH_RATE = 0.24
LOG2E = 1.4426950408889634

NX, NY, NZ = 4, 4, 8
TILES, SLOT = 48, 6
SLOT_ROWS, OWNERS = 80, 5
AWAY = (2, 1, 3, 0)

XF, CR = 0, 6
YR = CR + 4
ZR = YR + 3
ZG = ZR + 7
YG = ZG + 7
CG = YG + 3
HALO = CG + 5
N_SEM = HALO + 4


def kernel(
    dist, fac_hbm, vel_hbm, wgt_hbm, rel_hbm, val, moved, phit,
    fac, vel, wgt, rel, picks, lhs, reach, scaled, spread_f, snd, rcv, inc, wmat, phi,
    stage, part, got_c, got_y, got_z, full, tmp, again, ld_sem, small_sem, ssem, rsem,
):
    gx = lax.axis_index("gx")
    vert = lax.axis_index("vert")
    y = vert // 16
    z = (vert // 2) % 8
    core = vert % 2

    def vert_of(y_, z_, core_):
        return y_ * 16 + z_ * 2 + core_

    def copy(src, dst, send, recv, x_, v_):
        return pltpu.make_async_remote_copy(
            src_ref=src, dst_ref=dst, send_sem=ssem.at[send], recv_sem=rsem.at[recv],
            device_id=(x_, v_), device_id_type=MESH,
        )

    def rows8(r):
        return pl.ds(pl.multiple_of(r * 8, 8), 8)

    def load(n):
        d, cols = n // 4, pl.ds(n % 4 * 1536, 1536)
        return pltpu.make_async_copy(dist.at[d, :, cols], val.at[d, :, cols], ld_sem.at[n])

    small = [
        pltpu.make_async_copy(src, dst, small_sem.at[n])
        for n, (src, dst) in enumerate(((fac_hbm, fac), (wgt_hbm, wgt), (vel_hbm, vel), (rel_hbm, rel)))
    ]
    for one_copy in small:
        one_copy.start()
    for r in range(8):
        load(r).start()

    barrier = pltpu.get_barrier_semaphore()

    def greet(x_, v_):
        pl.semaphore_signal(barrier, inc=1, device_id=(x_, v_), device_id_type=MESH)

    for t in range(1, NX):
        greet((gx + t) % NX, vert)
    greet(gx, vert_of(y, z, 1 - core))
    for t in range(1, NY):
        greet(gx, vert_of((y + t) % NY, z, core))
    for t in range(1, NZ):
        greet(gx, vert_of(y, (z + t) % NZ, core))
    has_left, has_right = gx > 0, gx < NX - 1
    halo_here = jnp.where(core == 1, has_left, has_right)
    halo_x = jnp.where(core == 1, gx - 1, gx + 1)
    halo_y = jnp.where(core == 1, NY - 1, 0)

    @pl.when(halo_here & (y != halo_y))
    def _():
        greet(halo_x, vert_of(halo_y, z, core))

    halo_source = ((core == 1) & (y == NY - 1) & has_right) | ((core == 0) & (y == 0) & has_left)

    lane = lax.broadcasted_iota(jnp.int32, (8, 128), 1)
    low = lane < 64

    def lanes2(a, b):
        return jnp.concatenate([a, b], axis=1)

    cell = lax.broadcasted_iota(jnp.int32, (96, 384), 0) % 32
    cell -= jnp.where(lax.broadcasted_iota(jnp.int32, (96, 384), 1) >= 192, 1, 0)
    for p in range(16):
        picks[:, p * 384 : (p + 1) * 384] = jnp.where(cell == 2 * p, 1.0, 0.0).astype(BF16)

    small[0].wait()
    f = lanes2(fac[0], fac[1])
    q = jnp.sqrt(1.0 - f * f)
    at = lax.broadcasted_iota(jnp.int32, (32, 128), 0)
    ahead = lax.broadcasted_iota(jnp.int32, (32, 128), 1) < 64

    def down(x, k):
        return jnp.where(at >= k, pltpu.roll(x, k, 0), 1.0)

    def up(x, k):
        return jnp.where(at < 32 - k, pltpu.roll(x, 32 - k, 0), 1.0)

    before, after = f, f
    for k in (1, 2, 4, 8, 16):
        before, after = before * down(before, k), after * up(after, k)
    to_edge = q * jnp.where(ahead, up(after, 1), down(before, 1))

    def exact(x, n, extra):
        hi = x.astype(BF16).astype(F32)
        mid = (x - hi).astype(BF16).astype(F32)
        turned = jnp.concatenate([hi, mid, x - hi - mid, extra], axis=0).T
        lhs[n * 128 : (n + 1) * 128, :] = turned.astype(BF16)
        return turned

    def spread(first, refs, unroll):
        def some(n, _):
            for k in range(unroll):
                p = n * unroll + k
                cols = pl.ds(pl.multiple_of(p * 384, 128), 384)
                rows = lhs[first * 128 : (first + len(refs)) * 128, 0:96]
                wide = jnp.dot(rows, picks[:, cols], preferred_element_type=F32)
                for m, ref in enumerate(refs):
                    ref[:, :, cols] = wide[m * 128 : (m + 1) * 128].reshape(2, 64, 384)
            return 0

        lax.fori_loop(0, 16 // unroll, some, 0)

    phi[...] = exact(to_edge, 0, after)

    for d in range(2):
        through = jnp.zeros((8, 128), F32)
        for r in range(8):
            through = jnp.where(lane == r, phi[d * 64 + r * 8 : d * 64 + r * 8 + 8, 96:97], through)
        snd[d, 0:8, :] = through

    def whole_row(r):
        return 8 + 8 * r

    def half_row(pair):
        return 72 + 8 * pair

    def leave(d):
        total = None
        for p in range(16):
            if p % 4 == 0:
                load(d * 4 + p // 4).wait()
            cols = slice(p * 384, (p + 1) * 384)
            weight = jnp.dot(lhs[d * 64 : d * 64 + 64, 0:96], picks[:, cols], preferred_element_type=F32)
            term = weight * val[d, :, cols]
            total = term if total is None else total + term
        halves = []
        for r in range(8):
            a, b, c = [total[8 * r : 8 * r + 8, j * 128 : (j + 1) * 128] for j in range(3)]
            rb = pltpu.roll(b, 64, 1)
            if d == 0:
                ra = pltpu.roll(a, 64, 1)
                snd[d, whole_row(r) : whole_row(r) + 8, :] = c + jnp.where(low, ra, rb)
                halves.append(b + ra)
            else:
                rc = pltpu.roll(c, 64, 1)
                snd[d, whole_row(r) : whole_row(r) + 8, :] = a + jnp.where(low, rb, rc)
                halves.append(b + rc)
        for pair in range(4):
            one, other = halves[pair], halves[pair + 4]
            if d == 0:
                both = jnp.where(low, pltpu.roll(one, 64, 1), other)
            else:
                both = jnp.where(low, one, pltpu.roll(other, 64, 1))
            snd[d, half_row(pair) : half_row(pair) + 8, :] = both

    def edge(direction, t, target):
        n = XF + direction * 3 + t - 1
        return copy(snd.at[direction], rcv.at[direction, t - 1], n, n, target, vert)

    def drain_x():
        for t in range(1, NX):
            @pl.when(gx + t < NX)
            def _():
                edge(0, t, (gx + t) % NX).wait_send()

            @pl.when(gx - t >= 0)
            def _():
                edge(1, t, (gx - t) % NX).wait_send()

    for d in range(2):
        leave(d)
        if d == 0:
            pl.semaphore_wait(barrier, 14 + jnp.where(halo_source, 3, 0))
        for t in (2, 1, 3):
            target = gx + t if d == 0 else gx - t

            @pl.when((target >= 0) & (target < NX))
            def _():
                edge(d, t, target).start()

    for one_copy in small[1:]:
        one_copy.wait()
    for n in range(4):
        for ref in (stage, part):
            ref[n * SLOT_ROWS + 72 : n * SLOT_ROWS + 80, :] = jnp.zeros((8, 128), F32)
    full[10 * SLOT_ROWS : 10 * SLOT_ROWS + 8, :] = jnp.zeros((8, 128), F32)
    wmat[...] = jnp.zeros_like(wmat)
    for k in range(13):
        row = lanes2(wgt[k, 0:1, :], wgt[k, 1:2, :])
        hi = row.astype(BF16).astype(F32)
        lo = row - hi
        wmat[k : k + 1, 0:128] = hi
        wmat[k : k + 1, 128:256] = hi
        wmat[16 + k : 17 + k, 0:128] = lo

    vx, vy, vz = [lanes2(vel[j, 0:1, :], vel[j, 1:2, :]) for j in range(3)]
    relax = lanes2(rel[0:1, :], rel[1:2, :])
    xx, yy, zz = vx * vx, vy * vy, vz * vz
    sq = xx + yy + zz
    one = jnp.ones_like(vx)
    feats = [vx * sq, vy * sq, vz * sq, xx, yy, zz, vx * vy, vx * vz, vy * vz, vx, vy, vz, one]
    phi[...] = jnp.zeros_like(phi)
    for n, feat in enumerate(feats):
        for base, term in ((0, feat * relax), (48, feat)):
            hi = term.astype(BF16).astype(F32)
            phi[base + n : base + n + 1, :] = hi
            phi[base + 16 + n : base + 17 + n, :] = hi
            phi[base + 32 + n : base + 33 + n, :] = term - hi
    phi[96:97, :] = 1.0 - relax
    phit[...] = phi[...].T

    exact(f, 1, f)
    exact(q, 2, q)
    exact(jnp.where(ahead, before, after), 3, f)
    spread(1, [spread_f, scaled, reach], 2)

    def sweep(r):
        rows = rows8(r)
        zero = jnp.zeros((8, 128), F32)
        ones = jnp.ones((8, 128), F32)

        def cols(t):
            return pl.ds(t * 128, 128)

        value = [[zero] * 3, [zero] * 3]
        rolls = [[zero, zero], [zero, zero]]
        f_near = [ones, ones]
        for step in range(16):
            for d in range(2):
                p = step if d == 0 else 15 - step
                f = [spread_f[d, rows, cols(3 * p + j)] for j in range(3)]
                first, second = (f[0], f[2]) if d == 0 else (f[2], f[0])
                near, far = first * f_near[d], second * first
                f_near[d] = second
                if d == 0:
                    gs = [near, jnp.where(low, near, far), far]
                else:
                    gs = [far, jnp.where(low, far, near), near]
                for j in (0, 1, 2) if d == 0 else (2, 1, 0):
                    t = 3 * p + j
                    s = scaled[d, rows, cols(t)] * val[d, rows, cols(t)]
                    two_off, one_off = rolls[d]
                    neighbour = jnp.where(low, two_off, one_off) if d == 0 else jnp.where(low, one_off, two_off)
                    rolls[d] = [one_off, pltpu.roll(s, 64, 1)]
                    value[d][j] = gs[j] * value[d][j] + (s + f[j] * neighbour)
                    val[d, rows, cols(t)] = value[d][j]

    def sweep_rows(r, _):
        sweep(r)
        return 0

    lax.fori_loop(0, 8, sweep_rows, 0)

    for t in range(1, NX):
        @pl.when(gx - t >= 0)
        def _():
            edge(0, t, (gx - t) % NX).wait_recv()

        @pl.when(gx + t < NX)
        def _():
            edge(1, t, (gx + t) % NX).wait_recv()

    def entering(d):
        def add(n, state):
            slot = gx - n - 1 if d == 0 else NX - 2 - gx - n
            products = rcv[d, slot, 0:8, :]
            through = [jnp.broadcast_to(products[:, r : r + 1], (8, 128)) for r in range(8)]
            new = []
            for r in range(8):
                new.append(through[r] * state[r] + rcv[d, slot, whole_row(r) : whole_row(r) + 8, :])
            for pair in range(4):
                mixed = jnp.where(low, through[pair], through[pair + 4])
                new.append(mixed * state[8 + pair] + rcv[d, slot, half_row(pair) : half_row(pair) + 8, :])
            return tuple(new)

        state = lax.fori_loop(0, gx if d == 0 else NX - 1 - gx, add, (jnp.zeros((8, 128), F32),) * 12)
        for pair in range(4):
            h = state[8 + pair]
            turned = pltpu.roll(h, 64, 1)
            for k in range(2):
                r = pair + 4 * k
                a = state[r]
                ra = pltpu.roll(a, 64, 1)
                at_low, at_high = (h, turned) if k == 0 else (turned, h)
                if d == 0:
                    tiles = (jnp.where(low, at_low, ra), jnp.where(low, ra, at_high), a)
                else:
                    tiles = (a, jnp.where(low, at_low, ra), jnp.where(low, ra, at_high))
                for j in range(3):
                    inc[d, 8 * r : 8 * r + 8, j * 128 : (j + 1) * 128] = tiles[j]

    entering(0)
    entering(1)

    weights = wmat[...].astype(BF16)

    def moments(slot, dst, dst_row):
        for half in range(2):
            cols = pl.ds(pl.multiple_of(slot * 768 + half * 384, 128), 384)
            swept = val[:, :, cols] + reach[:, :, cols] * inc[...]
            val[:, :, cols] = swept
            flat = swept.reshape(128, 384)
            hi = flat.astype(BF16)
            lo = (flat - hi.astype(F32)).astype(BF16)
            both = jnp.dot(weights, jnp.concatenate([hi, lo], axis=0), preferred_element_type=F32)
            total = both[0:16] + both[16:32]
            for j in range(3):
                dst[pl.ds(dst_row + (half * 3 + j) * 13, 13), :] = total[0:13, j * 128 : (j + 1) * 128]

    def slot_rows(n):
        return pl.ds(n * SLOT_ROWS, SLOT_ROWS)

    partner = vert_of(y, z, 1 - core)

    def to_core(n):
        return copy(stage.at[slot_rows(n), :], got_c.at[slot_rows(n), :], CR + n, CR + n, gx, partner)

    def other_half(n, _):
        moments((1 - core) * 4 + (y + AWAY[n]) % NY, stage, n * SLOT_ROWS)
        to_core(n).start()
        return 0

    for n in range(4):
        other_half(n, 0)

    def to_y(n):
        return copy(
            part.at[slot_rows(n), :], got_y.at[slot_rows(n), :], YR + n, YR + n, gx, vert_of((y + AWAY[n]) % NY, z, core)
        )

    def own_half(n, _):
        moments(core * 4 + (y + AWAY[n]) % NY, part, n * SLOT_ROWS)
        to_core(n).wait_recv()
        part[slot_rows(n), :] += got_c[slot_rows(n), :]

        if n < 3:
            to_y(n).start()

    for n in range(4):
        own_half(n, 0)
    for n in range(3):
        to_y(n).wait_recv()
        part[slot_rows(3), :] += got_y[slot_rows(n), :]

    def drain_sums():
        for n in range(4):
            to_core(n).wait_send()
        for n in range(3):
            to_y(n).wait_send()

    def tile_rows(n):
        return pl.ds(pl.multiple_of(n * 16, 16), 16)

    mine = core * 4 + y
    own_row = (1 + mine) * SLOT_ROWS

    def to_z(n):
        peer = (z + n + 1) % NZ
        return copy(
            part.at[pl.ds(pl.multiple_of(3 * SLOT_ROWS + peer * 16, 16), 16), :], got_z.at[tile_rows(n), :],
            ZR + n, ZR + n, gx, vert_of(y, peer, core),
        )

    def from_owner(n, owner, target):
        tile = pl.ds(pl.multiple_of(own_row + owner * 16, 16), 16)
        return copy(full.at[tile, :], full.at[tile, :], ZG + n, ZG + n, gx, vert_of(y, target, core))

    def drain_z():
        for n in range(7):
            @pl.when((z + n + 1) % NZ < OWNERS)
            def _():
                to_z(n).wait_send()

    far_first = (3, 2, 4, 1, 5, 0, 6)
    for n in far_first:
        @pl.when((z + n + 1) % NZ < OWNERS)
        def _():
            to_z(n).start()

    @pl.when(z < OWNERS)
    def _():
        total = part[pl.ds(pl.multiple_of(3 * SLOT_ROWS + z * 16, 16), 16), :]
        for n in range(7):
            copy(got_z.at[tile_rows(n), :], got_z.at[tile_rows(n), :], ZR + n, ZR + n, gx, vert).wait_recv()
            total += got_z[tile_rows(n), :]
        full[pl.ds(pl.multiple_of(own_row + z * 16, 16), 16), :] = total
        for n in far_first:
            from_owner(n, z, (z + n + 1) % NZ).start()

    for n in range(7):
        owner = (z + NZ - n - 1) % NZ

        @pl.when(owner < OWNERS)
        def _():
            from_owner(n, owner, z).wait_recv()

    def slot_of(n):
        return pl.ds(pl.multiple_of((1 + n) * SLOT_ROWS, SLOT_ROWS), SLOT_ROWS)

    def gather_y(n, slot):
        return copy(
            full.at[slot_of(slot), :], full.at[slot_of(slot), :], YG + n, YG + n, gx, vert_of((y + n + 1) % NY, z, core)
        )

    halo_slot = jnp.where(core == 1, -1, 8)

    def send_halo(n):
        return copy(
            full.at[slot_of(mine), :], full.at[slot_of(halo_slot), :], HALO + n, HALO,
            jnp.where(core == 1, gx + 1, gx - 1), vert_of((y + n) % NY, z, core),
        )

    def gather_core(n, slot):
        return copy(full.at[slot_of(slot), :], full.at[slot_of(slot), :], CG + n, CG + n, gx, partner)

    @pl.when(halo_source)
    def _():
        for n in (2, 1, 3, 0):
            send_halo(n).start()

    for n in (1, 0, 2):
        gather_y(n, mine).start()

    gather_core(3, mine).start()
    for n in (0, 2, 1):
        slot = core * 4 + (y + NY - n - 1) % NY
        gather_y(n, slot).wait_recv()
        gather_core(n, slot).start()

    @pl.when(halo_here)
    def _():
        copy(full.at[slot_of(halo_slot), :], full.at[slot_of(halo_slot), :], HALO, HALO, gx, vert).wait_recv()
        gather_core(4, halo_slot).start()

    nothing = jnp.zeros((SLOT_ROWS, 128), F32)

    @pl.when(jnp.logical_not(has_left))
    def _():
        full[slot_of(-1), :] = nothing

    @pl.when(jnp.logical_not(has_right))
    def _():
        full[slot_of(8), :] = nothing

    for n in range(4):
        gather_core(n, (1 - core) * 4 + (y + NY - n - 1) % NY).wait_recv()

    other_halo = jnp.where(core == 1, 8, -1)

    @pl.when(jnp.where(core == 1, has_right, has_left))
    def _():
        gather_core(4, other_halo).wait_recv()

    for n in range(3):
        gather_y(n, mine).wait_send()

    @pl.when(halo_source)
    def _():
        for n in range(4):
            send_halo(n).wait_send()

    for n in range(4):
        gather_core(n, core * 4 + (y + NY - n - 1) % NY).wait_send()

    @pl.when(halo_here)
    def _():
        gather_core(4, halo_slot).wait_send()

    @pl.when(z < OWNERS)
    def _():
        for n in range(7):
            from_owner(n, z, (z + n + 1) % NZ).wait_send()

    left_flag = jnp.where(has_left, 1.0, 0.0).astype(F32)
    right_flag = jnp.where(has_right, 1.0, 0.0).astype(F32)

    def smooth(src, dst, first, last, skip=0):
        def get(t):
            if t < 0 or t > 59:
                return [jnp.zeros((8, 128), F32)] * 2
            row = t // SLOT * SLOT_ROWS + t % SLOT * 13 if src is full else t * 16
            return [src[row + 8 * h : row + 8 * h + 8, :] for h in range(2)]

        def rolled(t):
            return [pltpu.roll(m, 64, 1) for m in get(t)]

        around = {t: rolled(t) for t in range(first - 2, first + 2)}
        for t in range(first, last + 1):
            around[t + 2] = rolled(t + 2)
            here = get(t)
            density = jnp.broadcast_to(here[0][0:1, :], (8, 128))
            coef = SMOOTH_RATE / (1.0 + density * density)
            if t < SLOT:
                coef = coef * left_flag
            if t >= 54:
                coef = coef * right_flag
            for h in range(2):
                before = jnp.where(low, around[t - 2][h], around[t - 1][h])
                after = jnp.where(low, around[t + 1][h], around[t + 2][h])
                dst[(t - skip) * 16 + 8 * h : (t - skip) * 16 + 8 * h + 8, :] = here[h] + coef * (before + after - 2.0 * here[h])
            del around[t - 2]

    smooth(full, tmp, 1, 58)
    smooth(tmp, again, 3, 56)
    smooth(again, tmp, 4, 55)
    smooth(tmp, moved, 6, 53, 6)
    drain_x()
    drain_sums()
    drain_z()


def relax_kernel(val, moved, phit, out, mac, mac_buf, coef_f, coef_l, keep, buf, out_sem, mac_sem):
    for t in range(TILES):
        mac_buf[:, t * 128 : (t + 1) * 128] = moved[t * 16 : t * 16 + 13, :]
    mac_copy = pltpu.make_async_copy(mac_buf, mac, mac_sem)
    mac_copy.start()

    def row(k):
        return jnp.tanh(moved[pl.ds(k, TILES, stride=16), :])

    density = 1.0 + 0.5 * row(0)
    ux, uy, uz = 0.5 * row(1), 0.5 * row(2), 0.5 * row(3)
    g = 1.0 / (1.0 + 0.5 * row(4))
    s0, s1, s2, s3, s4 = [0.2 * row(5 + j) for j in range(5)]
    qx, qy, qz = [0.2 * row(10 + j) for j in range(3)]
    front = density * g * jnp.sqrt(g)
    h = 0.5 * g
    sxx, syy = 0.5 * s3, 0.5 * s4
    szz = -(sxx + syy)
    square = ux * ux + uy * uy + uz * uz
    a = qx * ux + qy * uy + qz * uz
    b = h * square - 2.5
    ah = a * h
    scale = front * g
    quad = (
        ux * (sxx * ux + s0 * uy + s1 * uz) + uy * (syy * uy + s2 * uz) + szz * uz * uz
    )
    values_f = [
        scale * h * qx, scale * h * qy, scale * h * qz,
        scale * (sxx - g * qx * ux - ah),
        scale * (syy - g * qy * uy - ah),
        scale * (szz - g * qz * uz - ah),
        scale * (s0 - g * (qx * uy + qy * ux)),
        scale * (s1 - g * (qx * uz + qz * ux)),
        scale * (s2 - g * (qy * uz + qz * uy)),
        scale * (b * qx + 2.0 * ah * ux - (2.0 * sxx * ux + s0 * uy + s1 * uz)),
        scale * (b * qy + 2.0 * ah * uy - (s0 * ux + 2.0 * syy * uy + s2 * uz)),
        scale * (b * qz + 2.0 * ah * uz - (s1 * ux + s2 * uy + 2.0 * szz * uz)),
        front + scale * (quad - a * b),
    ]
    le = -LOG2E * h
    none = jnp.zeros_like(le)
    values_l = [none] * 3 + [le] * 3 + [none] * 3 + [-2.0 * le * ux, -2.0 * le * uy, -2.0 * le * uz, le * square]
    for n in range(16):
        coef_f[pl.ds(n, TILES, stride=16), :] = values_f[n] if n < 13 else none
        coef_l[pl.ds(n, TILES, stride=16), :] = values_l[n] if n < 13 else none

    lhs_f = phit[:, 0:48].astype(BF16)
    lhs_l = phit[:, 48:96].astype(BF16)
    keep[...] = jnp.broadcast_to(phit[:, 96:97], (128, 128))

    def split(ref, n):
        c = jnp.concatenate([ref[n * 96 + 16 * j : n * 96 + 16 * j + 16, :] for j in range(SLOT)], axis=1)
        hi = c.astype(BF16)
        lo = (c - hi.astype(F32)).astype(BF16)
        return jnp.concatenate([hi, lo, hi], axis=0)

    def put(n):
        return pltpu.make_async_copy(buf.at[n], out.at[:, :, n * 768 : (n + 1) * 768], out_sem.at[n])

    for n in range(8):
        poly = jnp.dot(lhs_f, split(coef_f, n), preferred_element_type=F32)
        power = jnp.dot(lhs_l, split(coef_l, n), preferred_element_type=F32)
        for j in range(SLOT):
            part = slice(j * 128, (j + 1) * 128)
            swept = val[:, :, n * 768 + j * 128 : n * 768 + (j + 1) * 128].reshape(128, 128)
            buf[n, :, :, part] = (keep[...] * swept + poly[:, part] * jnp.exp2(power[:, part])).reshape(2, 64, 128)
        put(n).start()
    for n in range(8):
        put(n).wait()
    mac_copy.wait()


def per_device(dist, factors, velocity, weights, relax):
    vmem = pl.BlockSpec(memory_space=pltpu.VMEM)
    hbm = pl.BlockSpec(memory_space=pltpu.HBM)
    operands = (dist, jnp.transpose(factors, (0, 2, 1)), velocity, weights, relax)
    swept, moved, phit = pl.pallas_call(
        kernel,
        out_shape=(
            jax.ShapeDtypeStruct((2, 64, 6144), F32),
            jax.ShapeDtypeStruct((TILES * 16, 128), F32),
            jax.ShapeDtypeStruct((128, 128), F32),
        ),
        in_specs=[hbm] * 5,
        out_specs=(vmem, vmem, vmem),
        scratch_shapes=[
            pltpu.VMEM((2, 32, 64), F32),
            pltpu.VMEM((3, 2, 64), F32),
            pltpu.VMEM((13, 2, 64), F32),
            pltpu.VMEM((2, 64), F32),
            pltpu.VMEM((96, 6144), BF16),
            pltpu.VMEM((512, 128), BF16),
            pltpu.VMEM((2, 64, 6144), F32),
            pltpu.VMEM((2, 64, 6144), F32),
            pltpu.VMEM((2, 64, 6144), F32),
            pltpu.VMEM((2, 104, 128), F32),
            pltpu.VMEM((2, 3, 104, 128), F32),
            pltpu.VMEM((2, 64, 384), F32),
            pltpu.VMEM((32, 256), F32),
            pltpu.VMEM((128, 128), F32),
            pltpu.VMEM((4 * SLOT_ROWS, 128), F32),
            pltpu.VMEM((4 * SLOT_ROWS, 128), F32),
            pltpu.VMEM((4 * SLOT_ROWS, 128), F32),
            pltpu.VMEM((3 * SLOT_ROWS, 128), F32),
            pltpu.VMEM((7 * 16, 128), F32),
            pltpu.VMEM((10 * SLOT_ROWS + 8, 128), F32),
            pltpu.VMEM((60 * 16, 128), F32),
            pltpu.VMEM((60 * 16, 128), F32),
            pltpu.SemaphoreType.DMA((8,)),
            pltpu.SemaphoreType.DMA((4,)),
            pltpu.SemaphoreType.DMA((N_SEM,)),
            pltpu.SemaphoreType.DMA((N_SEM,)),
        ],
        compiler_params=pltpu.CompilerParams(
            collective_id=0, has_side_effects=True, vmem_limit_bytes=40 * 2**20
        ),
    )(*[pltpu.with_memory_space_constraint(x, pltpu.HBM) for x in operands])
    return pl.pallas_call(
        relax_kernel,
        out_shape=(
            jax.ShapeDtypeStruct((2, 64, 6144), F32),
            jax.ShapeDtypeStruct((13, 6144), F32),
        ),
        in_specs=[vmem] * 3,
        out_specs=(hbm, hbm),
        scratch_shapes=[
            pltpu.VMEM((13, 6144), F32),
            pltpu.VMEM((TILES * 16, 128), F32),
            pltpu.VMEM((TILES * 16, 128), F32),
            pltpu.VMEM((128, 128), F32),
            pltpu.VMEM((8, 2, 64, 768), F32),
            pltpu.SemaphoreType.DMA((8,)),
            pltpu.SemaphoreType.DMA,
        ],
        compiler_params=pltpu.CompilerParams(vmem_limit_bytes=32 * 2**20),
    )(swept, moved, phit)


def solution(mesh):
    return jax.shard_map(
        per_device,
        mesh=mesh,
        in_specs=(
            P(None, "vert", "gx"),
            P(None, "vert", "gx"),
            P(None, None, "vert"),
            P(None, None, "vert"),
            P(None, "vert"),
        ),
        out_specs=(P(None, "vert", "gx"), P(None, "gx")),
        check_vma=False,
    )
```

```python
import functools

import jax
import jax.numpy as jnp
from jax import lax
from jax.experimental import pallas as pl
from jax.experimental.pallas import tpu as pltpu
from jax.sharding import PartitionSpec as P

MESH = pl.DeviceIdType.MESH
F32, BF16 = jnp.float32, jnp.bfloat16
SMOOTH_RATE = 0.24
LOG2E = 1.4426950408889634

NX, NY, NZ = 4, 4, 8
TILES, SLOT = 48, 6
SLOT_ROWS, OWNERS = 80, 5
AWAY = ((2, 1), (2, 0), (1, 1), (3, 1), (1, 0), (3, 0), (0, 1), (0, 0))

XF, CR = 0, 6
ZR = CR + 7
ZG = ZR + 7
YG = ZG + 7
CG = YG + 7
HALO = CG + 1
N_SEM = HALO + 4


def kernel(
    dist, fac_hbm, vel_hbm, wgt_hbm, rel_hbm, val, moved, phit,
    fac, vel, wgt, rel, picks, lhs, reach, scaled, spread_f, snd, rcv, inc, wmat, phi,
    stage, part, got, got_z, full, tmp, again, ld_sem, small_sem, ssem, rsem,
):
    gx = lax.axis_index("gx")
    vert = lax.axis_index("vert")
    y = vert // 16
    z = (vert // 2) % 8
    core = vert % 2

    def vert_of(y_, z_, core_):
        return y_ * 16 + z_ * 2 + core_

    def copy(src, dst, send, recv, x_, v_):
        return pltpu.make_async_remote_copy(
            src_ref=src, dst_ref=dst, send_sem=ssem.at[send], recv_sem=rsem.at[recv],
            device_id=(x_, v_), device_id_type=MESH,
        )

    def rows8(r):
        return pl.ds(pl.multiple_of(r * 8, 8), 8)

    def load(n):
        d, cols = n // 4, pl.ds(n % 4 * 1536, 1536)
        return pltpu.make_async_copy(dist.at[d, :, cols], val.at[d, :, cols], ld_sem.at[n])

    small = [
        pltpu.make_async_copy(src, dst, small_sem.at[n])
        for n, (src, dst) in enumerate(((fac_hbm, fac), (wgt_hbm, wgt), (vel_hbm, vel), (rel_hbm, rel)))
    ]
    for one_copy in small:
        one_copy.start()
    for r in range(8):
        load(r).start()

    barrier = pltpu.get_barrier_semaphore()

    def greet(x_, v_):
        pl.semaphore_signal(barrier, inc=1, device_id=(x_, v_), device_id_type=MESH)

    for t in range(1, NX):
        greet((gx + t) % NX, vert)
    greet(gx, vert_of(y, z, 1 - core))
    for t in range(1, NY):
        for core_ in (core, 1 - core):
            greet(gx, vert_of((y + t) % NY, z, core_))
    for t in range(1, NZ):
        greet(gx, vert_of(y, (z + t) % NZ, core))
    has_left, has_right = gx > 0, gx < NX - 1
    halo_here = jnp.where(core == 1, has_left, has_right)
    halo_x = jnp.where(core == 1, gx - 1, gx + 1)
    halo_y = jnp.where(core == 1, NY - 1, 0)

    @pl.when(halo_here & (y != halo_y))
    def _():
        greet(halo_x, vert_of(halo_y, z, core))

    halo_source = ((core == 1) & (y == NY - 1) & has_right) | ((core == 0) & (y == 0) & has_left)

    lane = lax.broadcasted_iota(jnp.int32, (8, 128), 1)
    low = lane < 64

    def lanes2(a, b):
        return jnp.concatenate([a, b], axis=1)

    cell = lax.broadcasted_iota(jnp.int32, (96, 384), 0) % 32
    cell -= jnp.where(lax.broadcasted_iota(jnp.int32, (96, 384), 1) >= 192, 1, 0)
    for p in range(16):
        picks[:, p * 384 : (p + 1) * 384] = jnp.where(cell == 2 * p, 1.0, 0.0).astype(BF16)

    small[0].wait()
    f = lanes2(fac[0], fac[1])
    q = jnp.sqrt(1.0 - f * f)
    at = lax.broadcasted_iota(jnp.int32, (32, 128), 0)
    ahead = lax.broadcasted_iota(jnp.int32, (32, 128), 1) < 64

    def down(x, k):
        return jnp.where(at >= k, pltpu.roll(x, k, 0), 1.0)

    def up(x, k):
        return jnp.where(at < 32 - k, pltpu.roll(x, 32 - k, 0), 1.0)

    before, after = f, f
    for k in (1, 2, 4, 8, 16):
        before, after = before * down(before, k), after * up(after, k)
    to_edge = q * jnp.where(ahead, up(after, 1), down(before, 1))

    def exact(x, n, extra):
        hi = x.astype(BF16).astype(F32)
        mid = (x - hi).astype(BF16).astype(F32)
        turned = jnp.concatenate([hi, mid, x - hi - mid, extra], axis=0).T
        lhs[n * 128 : (n + 1) * 128, :] = turned.astype(BF16)
        return turned

    def spread(first, refs):
        for p in range(16):
            cols = slice(p * 384, (p + 1) * 384)
            rows = lhs[first * 128 : (first + len(refs)) * 128, 0:96]
            wide = jnp.dot(rows, picks[:, cols], preferred_element_type=F32)
            for m, ref in enumerate(refs):
                ref[:, :, cols] = wide[m * 128 : (m + 1) * 128].reshape(2, 64, 384)

    phi[...] = exact(to_edge, 0, after)

    for d in range(2):
        through = jnp.zeros((8, 128), F32)
        for r in range(8):
            through = jnp.where(lane == r, phi[d * 64 + r * 8 : d * 64 + r * 8 + 8, 96:97], through)
        snd[d, 0:8, :] = through

    def whole_row(r):
        return 8 + 8 * r

    def half_row(pair):
        return 72 + 8 * pair

    def leave(d):
        total = None
        for p in range(16):
            if p % 4 == 0:
                load(d * 4 + p // 4).wait()
            cols = slice(p * 384, (p + 1) * 384)
            weight = jnp.dot(lhs[d * 64 : d * 64 + 64, 0:96], picks[:, cols], preferred_element_type=F32)
            term = weight * val[d, :, cols]
            total = term if total is None else total + term
        halves = []
        for r in range(8):
            a, b, c = [total[8 * r : 8 * r + 8, j * 128 : (j + 1) * 128] for j in range(3)]
            rb = pltpu.roll(b, 64, 1)
            if d == 0:
                ra = pltpu.roll(a, 64, 1)
                snd[d, whole_row(r) : whole_row(r) + 8, :] = c + jnp.where(low, ra, rb)
                halves.append(b + ra)
            else:
                rc = pltpu.roll(c, 64, 1)
                snd[d, whole_row(r) : whole_row(r) + 8, :] = a + jnp.where(low, rb, rc)
                halves.append(b + rc)
        for pair in range(4):
            one, other = halves[pair], halves[pair + 4]
            if d == 0:
                both = jnp.where(low, pltpu.roll(one, 64, 1), other)
            else:
                both = jnp.where(low, one, pltpu.roll(other, 64, 1))
            snd[d, half_row(pair) : half_row(pair) + 8, :] = both

    def edge(direction, t, target):
        n = XF + direction * 3 + t - 1
        return copy(snd.at[direction], rcv.at[direction, t - 1], n, n, target, vert)

    def drain_x():
        for t in range(1, NX):
            @pl.when(gx + t < NX)
            def _():
                edge(0, t, (gx + t) % NX).wait_send()

            @pl.when(gx - t >= 0)
            def _():
                edge(1, t, (gx - t) % NX).wait_send()

    for d in range(2):
        leave(d)
        if d == 0:
            pl.semaphore_wait(barrier, 17 + jnp.where(halo_source, 3, 0))
        for t in (2, 1, 3):
            target = gx + t if d == 0 else gx - t

            @pl.when((target >= 0) & (target < NX))
            def _():
                edge(d, t, target).start()

    for one_copy in small[1:]:
        one_copy.wait()
    for n in range(7):
        stage[n * SLOT_ROWS + 72 : n * SLOT_ROWS + 80, :] = jnp.zeros((8, 128), F32)
    part[72:80, :] = jnp.zeros((8, 128), F32)
    full[10 * SLOT_ROWS : 10 * SLOT_ROWS + 8, :] = jnp.zeros((8, 128), F32)
    wmat[...] = jnp.zeros_like(wmat)
    for k in range(13):
        row = lanes2(wgt[k, 0:1, :], wgt[k, 1:2, :])
        hi = row.astype(BF16).astype(F32)
        lo = row - hi
        wmat[k : k + 1, 0:128] = hi
        wmat[k : k + 1, 128:256] = hi
        wmat[16 + k : 17 + k, 0:128] = lo

    vx, vy, vz = [lanes2(vel[j, 0:1, :], vel[j, 1:2, :]) for j in range(3)]
    relax = lanes2(rel[0:1, :], rel[1:2, :])
    xx, yy, zz = vx * vx, vy * vy, vz * vz
    sq = xx + yy + zz
    one = jnp.ones_like(vx)
    feats = [vx * sq, vy * sq, vz * sq, xx, yy, zz, vx * vy, vx * vz, vy * vz, vx, vy, vz, one]
    phi[...] = jnp.zeros_like(phi)
    for n, feat in enumerate(feats):
        for base, term in ((0, feat * relax), (48, feat)):
            hi = term.astype(BF16).astype(F32)
            phi[base + n : base + n + 1, :] = hi
            phi[base + 16 + n : base + 17 + n, :] = hi
            phi[base + 32 + n : base + 33 + n, :] = term - hi
    phi[96:97, :] = 1.0 - relax
    phit[...] = phi[...].T

    exact(f, 1, f)
    exact(q, 2, q)
    exact(jnp.where(ahead, before, after), 3, f)
    spread(1, [spread_f, scaled, reach])

    def sweep(r):
        rows = rows8(r)
        zero = jnp.zeros((8, 128), F32)
        ones = jnp.ones((8, 128), F32)

        def cols(t):
            return pl.ds(t * 128, 128)

        value = [[zero] * 3, [zero] * 3]
        rolls = [[zero, zero], [zero, zero]]
        f_near = [ones, ones]
        for step in range(16):
            for d in range(2):
                p = step if d == 0 else 15 - step
                f = [spread_f[d, rows, cols(3 * p + j)] for j in range(3)]
                first, second = (f[0], f[2]) if d == 0 else (f[2], f[0])
                near, far = first * f_near[d], second * first
                f_near[d] = second
                if d == 0:
                    gs = [near, jnp.where(low, near, far), far]
                else:
                    gs = [far, jnp.where(low, far, near), near]
                for j in (0, 1, 2) if d == 0 else (2, 1, 0):
                    t = 3 * p + j
                    s = scaled[d, rows, cols(t)] * val[d, rows, cols(t)]
                    two_off, one_off = rolls[d]
                    neighbour = jnp.where(low, two_off, one_off) if d == 0 else jnp.where(low, one_off, two_off)
                    rolls[d] = [one_off, pltpu.roll(s, 64, 1)]
                    value[d][j] = gs[j] * value[d][j] + (s + f[j] * neighbour)
                    val[d, rows, cols(t)] = value[d][j]

    def sweep_rows(r, _):
        sweep(r)
        return 0

    lax.fori_loop(0, 8, sweep_rows, 0)

    for t in range(1, NX):
        @pl.when(gx - t >= 0)
        def _():
            edge(0, t, (gx - t) % NX).wait_recv()

        @pl.when(gx + t < NX)
        def _():
            edge(1, t, (gx + t) % NX).wait_recv()

    def entering(d):
        def add(n, state):
            slot = gx - n - 1 if d == 0 else NX - 2 - gx - n
            products = rcv[d, slot, 0:8, :]
            through = [jnp.broadcast_to(products[:, r : r + 1], (8, 128)) for r in range(8)]
            new = []
            for r in range(8):
                new.append(through[r] * state[r] + rcv[d, slot, whole_row(r) : whole_row(r) + 8, :])
            for pair in range(4):
                mixed = jnp.where(low, through[pair], through[pair + 4])
                new.append(mixed * state[8 + pair] + rcv[d, slot, half_row(pair) : half_row(pair) + 8, :])
            return tuple(new)

        state = lax.fori_loop(0, gx if d == 0 else NX - 1 - gx, add, (jnp.zeros((8, 128), F32),) * 12)
        for pair in range(4):
            h = state[8 + pair]
            turned = pltpu.roll(h, 64, 1)
            for k in range(2):
                r = pair + 4 * k
                a = state[r]
                ra = pltpu.roll(a, 64, 1)
                at_low, at_high = (h, turned) if k == 0 else (turned, h)
                if d == 0:
                    tiles = (jnp.where(low, at_low, ra), jnp.where(low, ra, at_high), a)
                else:
                    tiles = (a, jnp.where(low, at_low, ra), jnp.where(low, ra, at_high))
                for j in range(3):
                    inc[d, 8 * r : 8 * r + 8, j * 128 : (j + 1) * 128] = tiles[j]

    entering(0)
    entering(1)

    weights = wmat[...].astype(BF16)

    def moments(slot, dst, dst_row):
        for half in range(2):
            cols = pl.ds(pl.multiple_of(slot * 768 + half * 384, 128), 384)
            swept = val[:, :, cols] + reach[:, :, cols] * inc[...]
            val[:, :, cols] = swept
            flat = swept.reshape(128, 384)
            hi = flat.astype(BF16)
            lo = (flat - hi.astype(F32)).astype(BF16)
            both = jnp.dot(weights, jnp.concatenate([hi, lo], axis=0), preferred_element_type=F32)
            total = both[0:16] + both[16:32]
            for j in range(3):
                dst[pl.ds(dst_row + (half * 3 + j) * 13, 13), :] = total[0:13, j * 128 : (j + 1) * 128]

    def slot_rows(n):
        return pl.ds(n * SLOT_ROWS, SLOT_ROWS)

    partner = vert_of(y, z, 1 - core)

    def to_slot(n):
        dy, dc = AWAY[n]
        target = vert_of((y + dy) % NY, z, (core + dc) % 2)
        return copy(stage.at[slot_rows(n), :], got.at[slot_rows(n), :], CR + n, CR + n, gx, target)

    for n, (dy, dc) in enumerate(AWAY):
        moments((core + dc) % 2 * 4 + (y + dy) % NY, stage if n < 7 else part, n % 7 * SLOT_ROWS)
        if n < 7:
            to_slot(n).start()
    for n in (6, 4, 5, 2, 3, 1, 0):
        to_slot(n).wait_recv()
        part[...] += got[slot_rows(n), :]

    def drain_sums():
        for n in range(7):
            to_slot(n).wait_send()

    def tile_rows(n):
        return pl.ds(pl.multiple_of(n * 16, 16), 16)

    mine = core * 4 + y
    own_row = (1 + mine) * SLOT_ROWS

    def to_z(n):
        peer = (z + n + 1) % NZ
        return copy(
            part.at[pl.ds(pl.multiple_of(peer * 16, 16), 16), :], got_z.at[tile_rows(n), :],
            ZR + n, ZR + n, gx, vert_of(y, peer, core),
        )

    def from_owner(n, owner, target):
        tile = pl.ds(pl.multiple_of(own_row + owner * 16, 16), 16)
        return copy(full.at[tile, :], full.at[tile, :], ZG + n, ZG + n, gx, vert_of(y, target, core))

    def drain_z():
        for n in range(7):
            @pl.when((z + n + 1) % NZ < OWNERS)
            def _():
                to_z(n).wait_send()

    far_first = (3, 2, 4, 1, 5, 0, 6)
    for n in far_first:
        @pl.when((z + n + 1) % NZ < OWNERS)
        def _():
            to_z(n).start()

    @pl.when(z < OWNERS)
    def _():
        total = part[pl.ds(pl.multiple_of(z * 16, 16), 16), :]
        for n in range(7):
            copy(got_z.at[tile_rows(n), :], got_z.at[tile_rows(n), :], ZR + n, ZR + n, gx, vert).wait_recv()
            total += got_z[tile_rows(n), :]
        full[pl.ds(pl.multiple_of(own_row + z * 16, 16), 16), :] = total
        for n in far_first:
            from_owner(n, z, (z + n + 1) % NZ).start()

    for n in range(7):
        owner = (z + NZ - n - 1) % NZ

        @pl.when(owner < OWNERS)
        def _():
            from_owner(n, owner, z).wait_recv()

    def slot_of(n):
        return pl.ds(pl.multiple_of((1 + n) * SLOT_ROWS, SLOT_ROWS), SLOT_ROWS)

    def gather(n, slot):
        dy, dc = AWAY[n]
        target = vert_of((y + dy) % NY, z, (core + dc) % 2)
        return copy(full.at[slot_of(slot), :], full.at[slot_of(slot), :], YG + n, YG + n, gx, target)

    def slot_from(n):
        dy, dc = AWAY[n]
        return (core + dc) % 2 * 4 + (y + NY - dy) % NY

    halo_slot = jnp.where(core == 1, -1, 8)

    def send_halo(n):
        return copy(
            full.at[slot_of(mine), :], full.at[slot_of(halo_slot), :], HALO + n, HALO,
            jnp.where(core == 1, gx + 1, gx - 1), vert_of((y + n) % NY, z, core),
        )

    def relay_halo(slot):
        return copy(full.at[slot_of(slot), :], full.at[slot_of(slot), :], CG, CG, gx, partner)

    @pl.when(halo_source)
    def _():
        for n in (2, 1, 3, 0):
            send_halo(n).start()

    for n in range(7):
        gather(n, mine).start()

    @pl.when(halo_here)
    def _():
        copy(full.at[slot_of(halo_slot), :], full.at[slot_of(halo_slot), :], HALO, HALO, gx, vert).wait_recv()
        relay_halo(halo_slot).start()

    nothing = jnp.zeros((SLOT_ROWS, 128), F32)

    @pl.when(jnp.logical_not(has_left))
    def _():
        full[slot_of(-1), :] = nothing

    @pl.when(jnp.logical_not(has_right))
    def _():
        full[slot_of(8), :] = nothing

    for n in range(7):
        gather(n, slot_from(n)).wait_recv()

    other_halo = jnp.where(core == 1, 8, -1)

    @pl.when(jnp.where(core == 1, has_right, has_left))
    def _():
        relay_halo(other_halo).wait_recv()

    for n in range(7):
        gather(n, mine).wait_send()

    @pl.when(halo_source)
    def _():
        for n in range(4):
            send_halo(n).wait_send()

    @pl.when(halo_here)
    def _():
        relay_halo(halo_slot).wait_send()

    @pl.when(z < OWNERS)
    def _():
        for n in range(7):
            from_owner(n, z, (z + n + 1) % NZ).wait_send()

    left_flag = jnp.where(has_left, 1.0, 0.0).astype(F32)
    right_flag = jnp.where(has_right, 1.0, 0.0).astype(F32)

    def smooth(src, dst, first, last, skip=0):
        def get(t):
            if t < 0 or t > 59:
                return [jnp.zeros((8, 128), F32)] * 2
            row = t // SLOT * SLOT_ROWS + t % SLOT * 13 if src is full else t * 16
            return [src[row + 8 * h : row + 8 * h + 8, :] for h in range(2)]

        def rolled(t):
            return [pltpu.roll(m, 64, 1) for m in get(t)]

        around = {t: rolled(t) for t in range(first - 2, first + 2)}
        for t in range(first, last + 1):
            around[t + 2] = rolled(t + 2)
            here = get(t)
            density = jnp.broadcast_to(here[0][0:1, :], (8, 128))
            coef = SMOOTH_RATE / (1.0 + density * density)
            if t < SLOT:
                coef = coef * left_flag
            if t >= 54:
                coef = coef * right_flag
            for h in range(2):
                before = jnp.where(low, around[t - 2][h], around[t - 1][h])
                after = jnp.where(low, around[t + 1][h], around[t + 2][h])
                dst[(t - skip) * 16 + 8 * h : (t - skip) * 16 + 8 * h + 8, :] = here[h] + coef * (before + after - 2.0 * here[h])
            del around[t - 2]

    smooth(full, tmp, 1, 58)
    smooth(tmp, again, 3, 56)
    smooth(again, tmp, 4, 55)
    smooth(tmp, moved, 6, 53, 6)
    drain_x()
    drain_sums()
    drain_z()


def relax_kernel(val, moved, phit, out, mac, mac_buf, coef_f, coef_l, keep, buf, out_sem, mac_sem):
    for t in range(TILES):
        mac_buf[:, t * 128 : (t + 1) * 128] = moved[t * 16 : t * 16 + 13, :]
    mac_copy = pltpu.make_async_copy(mac_buf, mac, mac_sem)
    mac_copy.start()

    def row(k):
        return jnp.tanh(moved[pl.ds(k, TILES, stride=16), :])

    density = 1.0 + 0.5 * row(0)
    ux, uy, uz = 0.5 * row(1), 0.5 * row(2), 0.5 * row(3)
    g = 1.0 / (1.0 + 0.5 * row(4))
    s0, s1, s2, s3, s4 = [0.2 * row(5 + j) for j in range(5)]
    qx, qy, qz = [0.2 * row(10 + j) for j in range(3)]
    front = density * g * jnp.sqrt(g)
    h = 0.5 * g
    sxx, syy = 0.5 * s3, 0.5 * s4
    szz = -(sxx + syy)
    square = ux * ux + uy * uy + uz * uz
    a = qx * ux + qy * uy + qz * uz
    b = h * square - 2.5
    ah = a * h
    scale = front * g
    quad = (
        ux * (sxx * ux + s0 * uy + s1 * uz) + uy * (syy * uy + s2 * uz) + szz * uz * uz
    )
    values_f = [
        scale * h * qx, scale * h * qy, scale * h * qz,
        scale * (sxx - g * qx * ux - ah),
        scale * (syy - g * qy * uy - ah),
        scale * (szz - g * qz * uz - ah),
        scale * (s0 - g * (qx * uy + qy * ux)),
        scale * (s1 - g * (qx * uz + qz * ux)),
        scale * (s2 - g * (qy * uz + qz * uy)),
        scale * (b * qx + 2.0 * ah * ux - (2.0 * sxx * ux + s0 * uy + s1 * uz)),
        scale * (b * qy + 2.0 * ah * uy - (s0 * ux + 2.0 * syy * uy + s2 * uz)),
        scale * (b * qz + 2.0 * ah * uz - (s1 * ux + s2 * uy + 2.0 * szz * uz)),
        front + scale * (quad - a * b),
    ]
    le = -LOG2E * h
    none = jnp.zeros_like(le)
    values_l = [none] * 3 + [le] * 3 + [none] * 3 + [-2.0 * le * ux, -2.0 * le * uy, -2.0 * le * uz, le * square]
    for n in range(16):
        coef_f[pl.ds(n, TILES, stride=16), :] = values_f[n] if n < 13 else none
        coef_l[pl.ds(n, TILES, stride=16), :] = values_l[n] if n < 13 else none

    lhs_f = phit[:, 0:48].astype(BF16)
    lhs_l = phit[:, 48:96].astype(BF16)
    keep[...] = jnp.broadcast_to(phit[:, 96:97], (128, 128))

    def split(ref, n):
        c = jnp.concatenate([ref[n * 96 + 16 * j : n * 96 + 16 * j + 16, :] for j in range(SLOT)], axis=1)
        hi = c.astype(BF16)
        lo = (c - hi.astype(F32)).astype(BF16)
        return jnp.concatenate([hi, lo, hi], axis=0)

    def put(n):
        return pltpu.make_async_copy(buf.at[n], out.at[:, :, n * 768 : (n + 1) * 768], out_sem.at[n])

    for n in range(8):
        poly = jnp.dot(lhs_f, split(coef_f, n), preferred_element_type=F32)
        power = jnp.dot(lhs_l, split(coef_l, n), preferred_element_type=F32)
        for j in range(SLOT):
            part = slice(j * 128, (j + 1) * 128)
            swept = val[:, :, n * 768 + j * 128 : n * 768 + (j + 1) * 128].reshape(128, 128)
            buf[n, :, :, part] = (keep[...] * swept + poly[:, part] * jnp.exp2(power[:, part])).reshape(2, 64, 128)
        put(n).start()
    for n in range(8):
        put(n).wait()
    mac_copy.wait()


def per_device(dist, factors, velocity, weights, relax):
    vmem = pl.BlockSpec(memory_space=pltpu.VMEM)
    hbm = pl.BlockSpec(memory_space=pltpu.HBM)
    operands = (dist, jnp.transpose(factors, (0, 2, 1)), velocity, weights, relax)
    swept, moved, phit = pl.pallas_call(
        kernel,
        out_shape=(
            jax.ShapeDtypeStruct((2, 64, 6144), F32),
            jax.ShapeDtypeStruct((TILES * 16, 128), F32),
            jax.ShapeDtypeStruct((128, 128), F32),
        ),
        in_specs=[hbm] * 5,
        out_specs=(vmem, vmem, vmem),
        scratch_shapes=[
            pltpu.VMEM((2, 32, 64), F32),
            pltpu.VMEM((3, 2, 64), F32),
            pltpu.VMEM((13, 2, 64), F32),
            pltpu.VMEM((2, 64), F32),
            pltpu.VMEM((96, 6144), BF16),
            pltpu.VMEM((512, 128), BF16),
            pltpu.VMEM((2, 64, 6144), F32),
            pltpu.VMEM((2, 64, 6144), F32),
            pltpu.VMEM((2, 64, 6144), F32),
            pltpu.VMEM((2, 104, 128), F32),
            pltpu.VMEM((2, 3, 104, 128), F32),
            pltpu.VMEM((2, 64, 384), F32),
            pltpu.VMEM((32, 256), F32),
            pltpu.VMEM((128, 128), F32),
            pltpu.VMEM((7 * SLOT_ROWS, 128), F32),
            pltpu.VMEM((SLOT_ROWS, 128), F32),
            pltpu.VMEM((7 * SLOT_ROWS, 128), F32),
            pltpu.VMEM((7 * 16, 128), F32),
            pltpu.VMEM((10 * SLOT_ROWS + 8, 128), F32),
            pltpu.VMEM((60 * 16, 128), F32),
            pltpu.VMEM((60 * 16, 128), F32),
            pltpu.SemaphoreType.DMA((8,)),
            pltpu.SemaphoreType.DMA((4,)),
            pltpu.SemaphoreType.DMA((N_SEM,)),
            pltpu.SemaphoreType.DMA((N_SEM,)),
        ],
        compiler_params=pltpu.CompilerParams(
            collective_id=0, has_side_effects=True, vmem_limit_bytes=40 * 2**20
        ),
    )(*[pltpu.with_memory_space_constraint(x, pltpu.HBM) for x in operands])
    return pl.pallas_call(
        relax_kernel,
        out_shape=(
            jax.ShapeDtypeStruct((2, 64, 6144), F32),
            jax.ShapeDtypeStruct((13, 6144), F32),
        ),
        in_specs=[vmem] * 3,
        out_specs=(hbm, hbm),
        scratch_shapes=[
            pltpu.VMEM((13, 6144), F32),
            pltpu.VMEM((TILES * 16, 128), F32),
            pltpu.VMEM((TILES * 16, 128), F32),
            pltpu.VMEM((128, 128), F32),
            pltpu.VMEM((8, 2, 64, 768), F32),
            pltpu.SemaphoreType.DMA((8,)),
            pltpu.SemaphoreType.DMA,
        ],
        compiler_params=pltpu.CompilerParams(vmem_limit_bytes=32 * 2**20),
    )(swept, moved, phit)


def solution(mesh):
    return jax.shard_map(
        per_device,
        mesh=mesh,
        in_specs=(
            P(None, "vert", "gx"),
            P(None, "vert", "gx"),
            P(None, None, "vert"),
            P(None, None, "vert"),
            P(None, "vert"),
        ),
        out_specs=(P(None, "vert", "gx"), P(None, "gx")),
        check_vma=False,
    )
```

```python
import functools

import jax
import jax.numpy as jnp
from jax import lax
from jax.experimental import pallas as pl
from jax.experimental.pallas import tpu as pltpu
from jax.sharding import PartitionSpec as P

MESH = pl.DeviceIdType.MESH
F32, BF16 = jnp.float32, jnp.bfloat16
SMOOTH_RATE = 0.24
LOG2E = 1.4426950408889634

NX, NY, NZ = 4, 4, 8
TILES, SLOT = 48, 6
SLOT_ROWS, OWNERS = 80, 5
AWAY = ((2, 1), (2, 0), (1, 1), (3, 1), (1, 0), (3, 0), (0, 1), (0, 0))

XF, CR = 0, 6
ZR = CR + 7
ZG = ZR + 7
YG = ZG + 7
CG = YG + 7
HALO = CG + 1
N_SEM = HALO + 4


def kernel(
    dist, fac_hbm, vel_hbm, wgt_hbm, rel_hbm, val, moved, phit,
    fac, vel, wgt, rel, picks, lhs, reach, scaled, spread_f, snd, rcv, inc, wmat, phi,
    stage, part, got, got_z, full, tmp, again, ld_sem, small_sem, ssem, rsem,
):
    gx = lax.axis_index("gx")
    vert = lax.axis_index("vert")
    y = vert // 16
    z = (vert // 2) % 8
    core = vert % 2

    def vert_of(y_, z_, core_):
        return y_ * 16 + z_ * 2 + core_

    def copy(src, dst, send, recv, x_, v_):
        return pltpu.make_async_remote_copy(
            src_ref=src, dst_ref=dst, send_sem=ssem.at[send], recv_sem=rsem.at[recv],
            device_id=(x_, v_), device_id_type=MESH,
        )

    def rows8(r):
        return pl.ds(pl.multiple_of(r * 8, 8), 8)

    def load(n):
        d, cols = n // 4, pl.ds(n % 4 * 1536, 1536)
        return pltpu.make_async_copy(dist.at[d, :, cols], val.at[d, :, cols], ld_sem.at[n])

    small = [
        pltpu.make_async_copy(src, dst, small_sem.at[n])
        for n, (src, dst) in enumerate(((fac_hbm, fac), (wgt_hbm, wgt), (vel_hbm, vel), (rel_hbm, rel)))
    ]
    for one_copy in small:
        one_copy.start()
    for r in (0, 4, 1, 5, 2, 6, 3, 7):
        load(r).start()

    barrier = pltpu.get_barrier_semaphore()

    def greet(x_, v_):
        pl.semaphore_signal(barrier, inc=1, device_id=(x_, v_), device_id_type=MESH)

    for t in range(1, NX):
        greet((gx + t) % NX, vert)
    greet(gx, vert_of(y, z, 1 - core))
    for t in range(1, NY):
        for core_ in (core, 1 - core):
            greet(gx, vert_of((y + t) % NY, z, core_))
    for t in range(1, NZ):
        greet(gx, vert_of(y, (z + t) % NZ, core))
    has_left, has_right = gx > 0, gx < NX - 1
    halo_here = jnp.where(core == 1, has_left, has_right)
    halo_x = jnp.where(core == 1, gx - 1, gx + 1)
    halo_y = jnp.where(core == 1, NY - 1, 0)

    @pl.when(halo_here & (y != halo_y))
    def _():
        greet(halo_x, vert_of(halo_y, z, core))

    halo_source = ((core == 1) & (y == NY - 1) & has_right) | ((core == 0) & (y == 0) & has_left)

    lane = lax.broadcasted_iota(jnp.int32, (8, 128), 1)
    low = lane < 64

    def lanes2(a, b):
        return jnp.concatenate([a, b], axis=1)

    cell = lax.broadcasted_iota(jnp.int32, (96, 384), 0) % 32
    cell -= jnp.where(lax.broadcasted_iota(jnp.int32, (96, 384), 1) >= 192, 1, 0)
    for p in range(16):
        picks[:, p * 384 : (p + 1) * 384] = jnp.where(cell == 2 * p, 1.0, 0.0).astype(BF16)

    small[0].wait()
    f = lanes2(fac[0], fac[1])
    q = jnp.sqrt(1.0 - f * f)
    at = lax.broadcasted_iota(jnp.int32, (32, 128), 0)
    ahead = lax.broadcasted_iota(jnp.int32, (32, 128), 1) < 64

    def down(x, k):
        return jnp.where(at >= k, pltpu.roll(x, k, 0), 1.0)

    def up(x, k):
        return jnp.where(at < 32 - k, pltpu.roll(x, 32 - k, 0), 1.0)

    before, after = f, f
    for k in (1, 2, 4, 8, 16):
        before, after = before * down(before, k), after * up(after, k)
    to_edge = q * jnp.where(ahead, up(after, 1), down(before, 1))

    def exact(x, n, extra):
        hi = x.astype(BF16).astype(F32)
        mid = (x - hi).astype(BF16).astype(F32)
        turned = jnp.concatenate([hi, mid, x - hi - mid, extra], axis=0).T
        lhs[n * 128 : (n + 1) * 128, :] = turned.astype(BF16)
        return turned

    def spread(first, refs):
        for p in range(16):
            cols = slice(p * 384, (p + 1) * 384)
            rows = lhs[first * 128 : (first + len(refs)) * 128, 0:96]
            wide = jnp.dot(rows, picks[:, cols], preferred_element_type=F32)
            for m, ref in enumerate(refs):
                ref[:, :, cols] = wide[m * 128 : (m + 1) * 128].reshape(2, 64, 384)

    phi[...] = exact(to_edge, 0, after)

    for d in range(2):
        through = jnp.zeros((8, 128), F32)
        for r in range(8):
            through = jnp.where(lane == r, phi[d * 64 + r * 8 : d * 64 + r * 8 + 8, 96:97], through)
        snd[d, 0:8, :] = through

    def whole_row(r):
        return 8 + 8 * r

    def half_row(pair):
        return 72 + 8 * pair

    def leave():
        total = None
        for p in range(16):
            if p % 4 == 0:
                load(p // 4).wait()
                load(4 + p // 4).wait()
            cols = slice(p * 384, (p + 1) * 384)
            weight = jnp.dot(lhs[0:128, 0:64], picks[0:64, cols], preferred_element_type=F32)
            term = weight * val[:, :, cols].reshape(128, 384)
            total = term if total is None else total + term
        return total

    def pack(d, total):
        halves = []
        for r in range(8):
            a, b, c = [total[8 * r : 8 * r + 8, j * 128 : (j + 1) * 128] for j in range(3)]
            rb = pltpu.roll(b, 64, 1)
            if d == 0:
                ra = pltpu.roll(a, 64, 1)
                snd[d, whole_row(r) : whole_row(r) + 8, :] = c + jnp.where(low, ra, rb)
                halves.append(b + ra)
            else:
                rc = pltpu.roll(c, 64, 1)
                snd[d, whole_row(r) : whole_row(r) + 8, :] = a + jnp.where(low, rb, rc)
                halves.append(b + rc)
        for pair in range(4):
            one, other = halves[pair], halves[pair + 4]
            if d == 0:
                both = jnp.where(low, pltpu.roll(one, 64, 1), other)
            else:
                both = jnp.where(low, one, pltpu.roll(other, 64, 1))
            snd[d, half_row(pair) : half_row(pair) + 8, :] = both

    def edge(direction, t, target):
        n = XF + direction * 3 + t - 1
        return copy(snd.at[direction], rcv.at[direction, t - 1], n, n, target, vert)

    def drain_x():
        for t in range(1, NX):
            @pl.when(gx + t < NX)
            def _():
                edge(0, t, (gx + t) % NX).wait_send()

            @pl.when(gx - t >= 0)
            def _():
                edge(1, t, (gx - t) % NX).wait_send()

    leaving = leave()
    for d in range(2):
        pack(d, leaving[d * 64 : d * 64 + 64])
        if d == 0:
            pl.semaphore_wait(barrier, 17 + jnp.where(halo_source, 3, 0))
        for t in (2, 1, 3):
            target = gx + t if d == 0 else gx - t

            @pl.when((target >= 0) & (target < NX))
            def _():
                edge(d, t, target).start()

    for one_copy in small[1:]:
        one_copy.wait()
    for n in range(7):
        stage[n * SLOT_ROWS + 72 : n * SLOT_ROWS + 80, :] = jnp.zeros((8, 128), F32)
    part[72:80, :] = jnp.zeros((8, 128), F32)
    full[10 * SLOT_ROWS : 10 * SLOT_ROWS + 8, :] = jnp.zeros((8, 128), F32)
    wmat[...] = jnp.zeros_like(wmat)
    for k in range(13):
        row = lanes2(wgt[k, 0:1, :], wgt[k, 1:2, :])
        hi = row.astype(BF16).astype(F32)
        lo = row - hi
        wmat[k : k + 1, 0:128] = hi
        wmat[k : k + 1, 128:256] = hi
        wmat[16 + k : 17 + k, 0:128] = lo

    vx, vy, vz = [lanes2(vel[j, 0:1, :], vel[j, 1:2, :]) for j in range(3)]
    relax = lanes2(rel[0:1, :], rel[1:2, :])
    xx, yy, zz = vx * vx, vy * vy, vz * vz
    sq = xx + yy + zz
    one = jnp.ones_like(vx)
    feats = [vx * sq, vy * sq, vz * sq, xx, yy, zz, vx * vy, vx * vz, vy * vz, vx, vy, vz, one]
    phi[...] = jnp.zeros_like(phi)
    for n, feat in enumerate(feats):
        for base, term in ((0, feat * relax), (48, feat)):
            hi = term.astype(BF16).astype(F32)
            phi[base + n : base + n + 1, :] = hi
            phi[base + 16 + n : base + 17 + n, :] = hi
            phi[base + 32 + n : base + 33 + n, :] = term - hi
    phi[96:97, :] = 1.0 - relax
    phit[...] = phi[...].T

    exact(f, 1, f)
    exact(q, 2, q)
    exact(jnp.where(ahead, before, after), 3, f)
    spread(1, [spread_f, scaled, reach])

    def sweep(r):
        rows = rows8(r)
        zero = jnp.zeros((8, 128), F32)
        ones = jnp.ones((8, 128), F32)

        def cols(t):
            return pl.ds(t * 128, 128)

        value = [[zero] * 3, [zero] * 3]
        rolls = [[zero, zero], [zero, zero]]
        f_near = [ones, ones]
        for step in range(16):
            for d in range(2):
                p = step if d == 0 else 15 - step
                f = [spread_f[d, rows, cols(3 * p + j)] for j in range(3)]
                first, second = (f[0], f[2]) if d == 0 else (f[2], f[0])
                near, far = first * f_near[d], second * first
                f_near[d] = second
                if d == 0:
                    gs = [near, jnp.where(low, near, far), far]
                else:
                    gs = [far, jnp.where(low, far, near), near]
                for j in (0, 1, 2) if d == 0 else (2, 1, 0):
                    t = 3 * p + j
                    s = scaled[d, rows, cols(t)] * val[d, rows, cols(t)]
                    two_off, one_off = rolls[d]
                    neighbour = jnp.where(low, two_off, one_off) if d == 0 else jnp.where(low, one_off, two_off)
                    rolls[d] = [one_off, pltpu.roll(s, 64, 1)]
                    value[d][j] = gs[j] * value[d][j] + (s + f[j] * neighbour)
                    val[d, rows, cols(t)] = value[d][j]

    def sweep_rows(r, _):
        sweep(r)
        return 0

    lax.fori_loop(0, 8, sweep_rows, 0)

    for t in range(1, NX):
        @pl.when(gx - t >= 0)
        def _():
            edge(0, t, (gx - t) % NX).wait_recv()

        @pl.when(gx + t < NX)
        def _():
            edge(1, t, (gx + t) % NX).wait_recv()

    def entering(d):
        def add(n, state):
            slot = gx - n - 1 if d == 0 else NX - 2 - gx - n
            products = rcv[d, slot, 0:8, :]
            through = [jnp.broadcast_to(products[:, r : r + 1], (8, 128)) for r in range(8)]
            new = []
            for r in range(8):
                new.append(through[r] * state[r] + rcv[d, slot, whole_row(r) : whole_row(r) + 8, :])
            for pair in range(4):
                mixed = jnp.where(low, through[pair], through[pair + 4])
                new.append(mixed * state[8 + pair] + rcv[d, slot, half_row(pair) : half_row(pair) + 8, :])
            return tuple(new)

        state = lax.fori_loop(0, gx if d == 0 else NX - 1 - gx, add, (jnp.zeros((8, 128), F32),) * 12)
        for pair in range(4):
            h = state[8 + pair]
            turned = pltpu.roll(h, 64, 1)
            for k in range(2):
                r = pair + 4 * k
                a = state[r]
                ra = pltpu.roll(a, 64, 1)
                at_low, at_high = (h, turned) if k == 0 else (turned, h)
                if d == 0:
                    tiles = (jnp.where(low, at_low, ra), jnp.where(low, ra, at_high), a)
                else:
                    tiles = (a, jnp.where(low, at_low, ra), jnp.where(low, ra, at_high))
                for j in range(3):
                    inc[d, 8 * r : 8 * r + 8, j * 128 : (j + 1) * 128] = tiles[j]

    entering(0)
    entering(1)

    weights = wmat[...].astype(BF16)

    def moments(slot, dst, dst_row):
        for half in range(2):
            cols = pl.ds(pl.multiple_of(slot * 768 + half * 384, 128), 384)
            swept = val[:, :, cols] + reach[:, :, cols] * inc[...]
            val[:, :, cols] = swept
            flat = swept.reshape(128, 384)
            hi = flat.astype(BF16)
            lo = (flat - hi.astype(F32)).astype(BF16)
            both = jnp.dot(weights, jnp.concatenate([hi, lo], axis=0), preferred_element_type=F32)
            total = both[0:16] + both[16:32]
            for j in range(3):
                dst[pl.ds(dst_row + (half * 3 + j) * 13, 13), :] = total[0:13, j * 128 : (j + 1) * 128]

    def slot_rows(n):
        return pl.ds(n * SLOT_ROWS, SLOT_ROWS)

    partner = vert_of(y, z, 1 - core)

    def to_slot(n):
        dy, dc = AWAY[n]
        target = vert_of((y + dy) % NY, z, (core + dc) % 2)
        return copy(stage.at[slot_rows(n), :], got.at[slot_rows(n), :], CR + n, CR + n, gx, target)

    for n, (dy, dc) in enumerate(AWAY):
        moments((core + dc) % 2 * 4 + (y + dy) % NY, stage if n < 7 else part, n % 7 * SLOT_ROWS)
        if n < 7:
            to_slot(n).start()
    for n in (6, 4, 5, 2, 3, 1, 0):
        to_slot(n).wait_recv()
        part[...] += got[slot_rows(n), :]

    def drain_sums():
        for n in range(7):
            to_slot(n).wait_send()

    def tile_rows(n):
        return pl.ds(pl.multiple_of(n * 16, 16), 16)

    mine = core * 4 + y
    own_row = (1 + mine) * SLOT_ROWS

    def to_z(n):
        peer = (z + n + 1) % NZ
        return copy(
            part.at[pl.ds(pl.multiple_of(peer * 16, 16), 16), :], got_z.at[tile_rows(n), :],
            ZR + n, ZR + n, gx, vert_of(y, peer, core),
        )

    def from_owner(n, owner, target):
        tile = pl.ds(pl.multiple_of(own_row + owner * 16, 16), 16)
        return copy(full.at[tile, :], full.at[tile, :], ZG + n, ZG + n, gx, vert_of(y, target, core))

    def drain_z():
        for n in range(7):
            @pl.when((z + n + 1) % NZ < OWNERS)
            def _():
                to_z(n).wait_send()

    far_first = (3, 2, 4, 1, 5, 0, 6)
    for n in far_first:
        @pl.when((z + n + 1) % NZ < OWNERS)
        def _():
            to_z(n).start()

    @pl.when(z < OWNERS)
    def _():
        total = part[pl.ds(pl.multiple_of(z * 16, 16), 16), :]
        for n in range(7):
            copy(got_z.at[tile_rows(n), :], got_z.at[tile_rows(n), :], ZR + n, ZR + n, gx, vert).wait_recv()
            total += got_z[tile_rows(n), :]
        full[pl.ds(pl.multiple_of(own_row + z * 16, 16), 16), :] = total
        for n in far_first:
            from_owner(n, z, (z + n + 1) % NZ).start()

    for n in range(7):
        owner = (z + NZ - n - 1) % NZ

        @pl.when(owner < OWNERS)
        def _():
            from_owner(n, owner, z).wait_recv()

    def slot_of(n):
        return pl.ds(pl.multiple_of((1 + n) * SLOT_ROWS, SLOT_ROWS), SLOT_ROWS)

    def gather(n, slot):
        dy, dc = AWAY[n]
        target = vert_of((y + dy) % NY, z, (core + dc) % 2)
        return copy(full.at[slot_of(slot), :], full.at[slot_of(slot), :], YG + n, YG + n, gx, target)

    def slot_from(n):
        dy, dc = AWAY[n]
        return (core + dc) % 2 * 4 + (y + NY - dy) % NY

    halo_slot = jnp.where(core == 1, -1, 8)

    def send_halo(n):
        return copy(
            full.at[slot_of(mine), :], full.at[slot_of(halo_slot), :], HALO + n, HALO,
            jnp.where(core == 1, gx + 1, gx - 1), vert_of((y + n) % NY, z, core),
        )

    def relay_halo(slot):
        return copy(full.at[slot_of(slot), :], full.at[slot_of(slot), :], CG, CG, gx, partner)

    @pl.when(halo_source)
    def _():
        for n in (2, 1, 3, 0):
            send_halo(n).start()

    for n in range(7):
        gather(n, mine).start()

    @pl.when(halo_here)
    def _():
        copy(full.at[slot_of(halo_slot), :], full.at[slot_of(halo_slot), :], HALO, HALO, gx, vert).wait_recv()
        relay_halo(halo_slot).start()

    nothing = jnp.zeros((SLOT_ROWS, 128), F32)

    @pl.when(jnp.logical_not(has_left))
    def _():
        full[slot_of(-1), :] = nothing

    @pl.when(jnp.logical_not(has_right))
    def _():
        full[slot_of(8), :] = nothing

    for n in range(7):
        gather(n, slot_from(n)).wait_recv()

    other_halo = jnp.where(core == 1, 8, -1)

    @pl.when(jnp.where(core == 1, has_right, has_left))
    def _():
        relay_halo(other_halo).wait_recv()

    for n in range(7):
        gather(n, mine).wait_send()

    @pl.when(halo_source)
    def _():
        for n in range(4):
            send_halo(n).wait_send()

    @pl.when(halo_here)
    def _():
        relay_halo(halo_slot).wait_send()

    @pl.when(z < OWNERS)
    def _():
        for n in range(7):
            from_owner(n, z, (z + n + 1) % NZ).wait_send()

    left_flag = jnp.where(has_left, 1.0, 0.0).astype(F32)
    right_flag = jnp.where(has_right, 1.0, 0.0).astype(F32)

    def smooth(src, dst, first, last, skip=0):
        def get(t):
            if t < 0 or t > 59:
                return [jnp.zeros((8, 128), F32)] * 2
            row = t // SLOT * SLOT_ROWS + t % SLOT * 13 if src is full else t * 16
            return [src[row + 8 * h : row + 8 * h + 8, :] for h in range(2)]

        def rolled(t):
            return [pltpu.roll(m, 64, 1) for m in get(t)]

        around = {t: rolled(t) for t in range(first - 2, first + 2)}
        for t in range(first, last + 1):
            around[t + 2] = rolled(t + 2)
            here = get(t)
            density = jnp.broadcast_to(here[0][0:1, :], (8, 128))
            coef = SMOOTH_RATE / (1.0 + density * density)
            if t < SLOT:
                coef = coef * left_flag
            if t >= 54:
                coef = coef * right_flag
            for h in range(2):
                before = jnp.where(low, around[t - 2][h], around[t - 1][h])
                after = jnp.where(low, around[t + 1][h], around[t + 2][h])
                dst[(t - skip) * 16 + 8 * h : (t - skip) * 16 + 8 * h + 8, :] = here[h] + coef * (before + after - 2.0 * here[h])
            del around[t - 2]

    smooth(full, tmp, 1, 58)
    smooth(tmp, again, 3, 56)
    smooth(again, tmp, 4, 55)
    smooth(tmp, moved, 6, 53, 6)
    drain_x()
    drain_sums()
    drain_z()


def relax_kernel(val, moved, phit, out, mac, mac_buf, coef_f, coef_l, keep, buf, out_sem, mac_sem):
    for t in range(TILES):
        mac_buf[:, t * 128 : (t + 1) * 128] = moved[t * 16 : t * 16 + 13, :]
    mac_copy = pltpu.make_async_copy(mac_buf, mac, mac_sem)
    mac_copy.start()

    def row(k):
        return jnp.tanh(moved[pl.ds(k, TILES, stride=16), :])

    density = 1.0 + 0.5 * row(0)
    ux, uy, uz = 0.5 * row(1), 0.5 * row(2), 0.5 * row(3)
    g = 1.0 / (1.0 + 0.5 * row(4))
    s0, s1, s2, s3, s4 = [0.2 * row(5 + j) for j in range(5)]
    qx, qy, qz = [0.2 * row(10 + j) for j in range(3)]
    front = density * g * jnp.sqrt(g)
    h = 0.5 * g
    sxx, syy = 0.5 * s3, 0.5 * s4
    szz = -(sxx + syy)
    square = ux * ux + uy * uy + uz * uz
    a = qx * ux + qy * uy + qz * uz
    b = h * square - 2.5
    ah = a * h
    scale = front * g
    quad = (
        ux * (sxx * ux + s0 * uy + s1 * uz) + uy * (syy * uy + s2 * uz) + szz * uz * uz
    )
    values_f = [
        scale * h * qx, scale * h * qy, scale * h * qz,
        scale * (sxx - g * qx * ux - ah),
        scale * (syy - g * qy * uy - ah),
        scale * (szz - g * qz * uz - ah),
        scale * (s0 - g * (qx * uy + qy * ux)),
        scale * (s1 - g * (qx * uz + qz * ux)),
        scale * (s2 - g * (qy * uz + qz * uy)),
        scale * (b * qx + 2.0 * ah * ux - (2.0 * sxx * ux + s0 * uy + s1 * uz)),
        scale * (b * qy + 2.0 * ah * uy - (s0 * ux + 2.0 * syy * uy + s2 * uz)),
        scale * (b * qz + 2.0 * ah * uz - (s1 * ux + s2 * uy + 2.0 * szz * uz)),
        front + scale * (quad - a * b),
    ]
    le = -LOG2E * h
    none = jnp.zeros_like(le)
    values_l = [none] * 3 + [le] * 3 + [none] * 3 + [-2.0 * le * ux, -2.0 * le * uy, -2.0 * le * uz, le * square]
    for n in range(16):
        coef_f[pl.ds(n, TILES, stride=16), :] = values_f[n] if n < 13 else none
        coef_l[pl.ds(n, TILES, stride=16), :] = values_l[n] if n < 13 else none

    lhs_f = phit[:, 0:48].astype(BF16)
    lhs_l = phit[:, 48:96].astype(BF16)
    keep[...] = jnp.broadcast_to(phit[:, 96:97], (128, 128))

    def split(ref, n):
        c = jnp.concatenate([ref[n * 96 + 16 * j : n * 96 + 16 * j + 16, :] for j in range(SLOT)], axis=1)
        hi = c.astype(BF16)
        lo = (c - hi.astype(F32)).astype(BF16)
        return jnp.concatenate([hi, lo, hi], axis=0)

    def put(n):
        return pltpu.make_async_copy(buf.at[n], out.at[:, :, n * 768 : (n + 1) * 768], out_sem.at[n])

    for n in range(8):
        poly = jnp.dot(lhs_f, split(coef_f, n), preferred_element_type=F32)
        power = jnp.dot(lhs_l, split(coef_l, n), preferred_element_type=F32)
        for j in range(SLOT):
            part = slice(j * 128, (j + 1) * 128)
            swept = val[:, :, n * 768 + j * 128 : n * 768 + (j + 1) * 128].reshape(128, 128)
            buf[n, :, :, part] = (keep[...] * swept + poly[:, part] * jnp.exp2(power[:, part])).reshape(2, 64, 128)
        put(n).start()
    for n in range(8):
        put(n).wait()
    mac_copy.wait()


def per_device(dist, factors, velocity, weights, relax):
    vmem = pl.BlockSpec(memory_space=pltpu.VMEM)
    hbm = pl.BlockSpec(memory_space=pltpu.HBM)
    operands = (dist, jnp.transpose(factors, (0, 2, 1)), velocity, weights, relax)
    swept, moved, phit = pl.pallas_call(
        kernel,
        out_shape=(
            jax.ShapeDtypeStruct((2, 64, 6144), F32),
            jax.ShapeDtypeStruct((TILES * 16, 128), F32),
            jax.ShapeDtypeStruct((128, 128), F32),
        ),
        in_specs=[hbm] * 5,
        out_specs=(vmem, vmem, vmem),
        scratch_shapes=[
            pltpu.VMEM((2, 32, 64), F32),
            pltpu.VMEM((3, 2, 64), F32),
            pltpu.VMEM((13, 2, 64), F32),
            pltpu.VMEM((2, 64), F32),
            pltpu.VMEM((96, 6144), BF16),
            pltpu.VMEM((512, 128), BF16),
            pltpu.VMEM((2, 64, 6144), F32),
            pltpu.VMEM((2, 64, 6144), F32),
            pltpu.VMEM((2, 64, 6144), F32),
            pltpu.VMEM((2, 104, 128), F32),
            pltpu.VMEM((2, 3, 104, 128), F32),
            pltpu.VMEM((2, 64, 384), F32),
            pltpu.VMEM((32, 256), F32),
            pltpu.VMEM((128, 128), F32),
            pltpu.VMEM((7 * SLOT_ROWS, 128), F32),
            pltpu.VMEM((SLOT_ROWS, 128), F32),
            pltpu.VMEM((7 * SLOT_ROWS, 128), F32),
            pltpu.VMEM((7 * 16, 128), F32),
            pltpu.VMEM((10 * SLOT_ROWS + 8, 128), F32),
            pltpu.VMEM((60 * 16, 128), F32),
            pltpu.VMEM((60 * 16, 128), F32),
            pltpu.SemaphoreType.DMA((8,)),
            pltpu.SemaphoreType.DMA((4,)),
            pltpu.SemaphoreType.DMA((N_SEM,)),
            pltpu.SemaphoreType.DMA((N_SEM,)),
        ],
        compiler_params=pltpu.CompilerParams(
            collective_id=0, has_side_effects=True, vmem_limit_bytes=40 * 2**20
        ),
    )(*[pltpu.with_memory_space_constraint(x, pltpu.HBM) for x in operands])
    return pl.pallas_call(
        relax_kernel,
        out_shape=(
            jax.ShapeDtypeStruct((2, 64, 6144), F32),
            jax.ShapeDtypeStruct((13, 6144), F32),
        ),
        in_specs=[vmem] * 3,
        out_specs=(hbm, hbm),
        scratch_shapes=[
            pltpu.VMEM((13, 6144), F32),
            pltpu.VMEM((TILES * 16, 128), F32),
            pltpu.VMEM((TILES * 16, 128), F32),
            pltpu.VMEM((128, 128), F32),
            pltpu.VMEM((8, 2, 64, 768), F32),
            pltpu.SemaphoreType.DMA((8,)),
            pltpu.SemaphoreType.DMA,
        ],
        compiler_params=pltpu.CompilerParams(vmem_limit_bytes=32 * 2**20),
    )(swept, moved, phit)


def solution(mesh):
    return jax.shard_map(
        per_device,
        mesh=mesh,
        in_specs=(
            P(None, "vert", "gx"),
            P(None, "vert", "gx"),
            P(None, None, "vert"),
            P(None, None, "vert"),
            P(None, "vert"),
        ),
        out_specs=(P(None, "vert", "gx"), P(None, "gx")),
        check_vma=False,
    )
```

```python
import functools

import jax
import jax.numpy as jnp
from jax import lax
from jax.experimental import pallas as pl
from jax.experimental.pallas import tpu as pltpu
from jax.sharding import PartitionSpec as P

MESH = pl.DeviceIdType.MESH
F32, BF16 = jnp.float32, jnp.bfloat16
SMOOTH_RATE = 0.24
LOG2E = 1.4426950408889634

NX, NY, NZ = 4, 4, 8
TILES, SLOT = 48, 6
SLOT_ROWS, OWNERS = 80, 5
AWAY = ((2, 1), (2, 0), (1, 1), (3, 1), (1, 0), (3, 0), (0, 1), (0, 0))

XF, CR = 0, 6
ZR = CR + 7
ZG = ZR + 7
YG = ZG + 7
CG = YG + 7
HALO = CG + 1
N_SEM = HALO + 4


def kernel(
    dist, fac_hbm, vel_hbm, wgt_hbm, rel_hbm, val, moved, phit,
    fac, vel, wgt, rel, picks, lhs, reach, scaled, spread_f, snd, rcv, inc, wmat, phi,
    stage, part, got, got_z, full, tmp, again, ld_sem, small_sem, ssem, rsem,
):
    gx = lax.axis_index("gx")
    vert = lax.axis_index("vert")
    y = vert // 16
    z = (vert // 2) % 8
    core = vert % 2

    def vert_of(y_, z_, core_):
        return y_ * 16 + z_ * 2 + core_

    def copy(src, dst, send, recv, x_, v_):
        return pltpu.make_async_remote_copy(
            src_ref=src, dst_ref=dst, send_sem=ssem.at[send], recv_sem=rsem.at[recv],
            device_id=(x_, v_), device_id_type=MESH,
        )

    def rows8(r):
        return pl.ds(pl.multiple_of(r * 8, 8), 8)

    def load(n):
        d, cols = n // 4, pl.ds(n % 4 * 1536, 1536)
        return pltpu.make_async_copy(dist.at[d, :, cols], val.at[d, :, cols], ld_sem.at[n])

    small = [
        pltpu.make_async_copy(src, dst, small_sem.at[n])
        for n, (src, dst) in enumerate(((fac_hbm, fac), (wgt_hbm, wgt), (vel_hbm, vel), (rel_hbm, rel)))
    ]
    for one_copy in small:
        one_copy.start()
    for r in (0, 4, 1, 5, 2, 6, 3, 7):
        load(r).start()

    barrier = pltpu.get_barrier_semaphore()

    def greet(x_, v_):
        pl.semaphore_signal(barrier, inc=1, device_id=(x_, v_), device_id_type=MESH)

    for t in range(1, NX):
        greet((gx + t) % NX, vert)
    greet(gx, vert_of(y, z, 1 - core))
    for t in range(1, NY):
        for core_ in (core, 1 - core):
            greet(gx, vert_of((y + t) % NY, z, core_))
    for t in range(1, NZ):
        greet(gx, vert_of(y, (z + t) % NZ, core))
    has_left, has_right = gx > 0, gx < NX - 1
    halo_here = jnp.where(core == 1, has_left, has_right)
    halo_x = jnp.where(core == 1, gx - 1, gx + 1)
    halo_y = jnp.where(core == 1, NY - 1, 0)

    @pl.when(halo_here & (y != halo_y))
    def _():
        greet(halo_x, vert_of(halo_y, z, core))

    halo_source = ((core == 1) & (y == NY - 1) & has_right) | ((core == 0) & (y == 0) & has_left)

    lane = lax.broadcasted_iota(jnp.int32, (8, 128), 1)
    low = lane < 64

    def lanes2(a, b):
        return jnp.concatenate([a, b], axis=1)

    cell = lax.broadcasted_iota(jnp.int32, (96, 384), 0) % 32
    cell -= jnp.where(lax.broadcasted_iota(jnp.int32, (96, 384), 1) >= 192, 1, 0)
    for p in range(16):
        picks[:, p * 384 : (p + 1) * 384] = jnp.where(cell == 2 * p, 1.0, 0.0).astype(BF16)

    small[0].wait()
    f = lanes2(fac[0], fac[1])
    q = jnp.sqrt(1.0 - f * f)
    at = lax.broadcasted_iota(jnp.int32, (32, 128), 0)
    ahead = lax.broadcasted_iota(jnp.int32, (32, 128), 1) < 64

    def down(x, k):
        return jnp.where(at >= k, pltpu.roll(x, k, 0), 1.0)

    def up(x, k):
        return jnp.where(at < 32 - k, pltpu.roll(x, 32 - k, 0), 1.0)

    before, after = f, f
    for k in (1, 2, 4, 8, 16):
        before, after = before * down(before, k), after * up(after, k)
    to_edge = q * jnp.where(ahead, up(after, 1), down(before, 1))

    def exact(x, n, extra):
        hi = x.astype(BF16).astype(F32)
        mid = (x - hi).astype(BF16).astype(F32)
        turned = jnp.concatenate([hi, mid, x - hi - mid, extra], axis=0).T
        lhs[n * 128 : (n + 1) * 128, :] = turned.astype(BF16)
        return turned

    def spread(first, refs):
        for p in range(16):
            cols = slice(p * 384, (p + 1) * 384)
            rows = lhs[first * 128 : (first + len(refs)) * 128, 0:96]
            wide = jnp.dot(rows, picks[:, cols], preferred_element_type=F32)
            for m, ref in enumerate(refs):
                ref[:, :, cols] = wide[m * 128 : (m + 1) * 128].reshape(2, 64, 384)

    phi[...] = exact(to_edge, 0, after)

    for d in range(2):
        through = jnp.zeros((8, 128), F32)
        for r in range(8):
            through = jnp.where(lane == r, phi[d * 64 + r * 8 : d * 64 + r * 8 + 8, 96:97], through)
        snd[d, 0:8, :] = through

    def whole_row(r):
        return 8 + 8 * r

    def half_row(pair):
        return 72 + 8 * pair

    def leave():
        total = None
        for p in range(16):
            if p % 4 == 0:
                load(p // 4).wait()
                load(4 + p // 4).wait()
            cols = slice(p * 384, (p + 1) * 384)
            weight = jnp.dot(lhs[0:128, 0:64], picks[0:64, cols], preferred_element_type=F32)
            term = weight * val[:, :, cols].reshape(128, 384)
            total = term if total is None else total + term
        return total

    def pack(d, total):
        halves = []
        for r in range(8):
            a, b, c = [total[8 * r : 8 * r + 8, j * 128 : (j + 1) * 128] for j in range(3)]
            rb = pltpu.roll(b, 64, 1)
            if d == 0:
                ra = pltpu.roll(a, 64, 1)
                snd[d, whole_row(r) : whole_row(r) + 8, :] = c + jnp.where(low, ra, rb)
                halves.append(b + ra)
            else:
                rc = pltpu.roll(c, 64, 1)
                snd[d, whole_row(r) : whole_row(r) + 8, :] = a + jnp.where(low, rb, rc)
                halves.append(b + rc)
        for pair in range(4):
            one, other = halves[pair], halves[pair + 4]
            if d == 0:
                both = jnp.where(low, pltpu.roll(one, 64, 1), other)
            else:
                both = jnp.where(low, one, pltpu.roll(other, 64, 1))
            snd[d, half_row(pair) : half_row(pair) + 8, :] = both

    def edge(direction, t, target):
        n = XF + direction * 3 + t - 1
        return copy(snd.at[direction], rcv.at[direction, t - 1], n, n, target, vert)

    def drain_x():
        for t in range(1, NX):
            @pl.when(gx + t < NX)
            def _():
                edge(0, t, (gx + t) % NX).wait_send()

            @pl.when(gx - t >= 0)
            def _():
                edge(1, t, (gx - t) % NX).wait_send()

    leaving = leave()
    for d in range(2):
        pack(d, leaving[d * 64 : d * 64 + 64])
        if d == 0:
            pl.semaphore_wait(barrier, 17 + jnp.where(halo_source, 3, 0))
        for t in (2, 1, 3):
            target = gx + t if d == 0 else gx - t

            @pl.when((target >= 0) & (target < NX))
            def _():
                edge(d, t, target).start()

    for one_copy in small[1:]:
        one_copy.wait()
    for n in range(7):
        stage[n * SLOT_ROWS + 72 : n * SLOT_ROWS + 80, :] = jnp.zeros((8, 128), F32)
    part[72:80, :] = jnp.zeros((8, 128), F32)
    full[10 * SLOT_ROWS : 10 * SLOT_ROWS + 8, :] = jnp.zeros((8, 128), F32)
    wmat[...] = jnp.zeros_like(wmat)
    for k in range(13):
        row = lanes2(wgt[k, 0:1, :], wgt[k, 1:2, :])
        hi = row.astype(BF16).astype(F32)
        lo = row - hi
        wmat[k : k + 1, 0:128] = hi
        wmat[k : k + 1, 128:256] = hi
        wmat[16 + k : 17 + k, 0:128] = lo

    vx, vy, vz = [lanes2(vel[j, 0:1, :], vel[j, 1:2, :]) for j in range(3)]
    relax = lanes2(rel[0:1, :], rel[1:2, :])
    xx, yy, zz = vx * vx, vy * vy, vz * vz
    sq = xx + yy + zz
    one = jnp.ones_like(vx)
    feats = [vx * sq, vy * sq, vz * sq, xx, yy, zz, vx * vy, vx * vz, vy * vz, vx, vy, vz, one]
    phi[...] = jnp.zeros_like(phi)
    for n, feat in enumerate(feats):
        for base, term in ((0, feat * relax), (48, feat)):
            hi = term.astype(BF16).astype(F32)
            phi[base + n : base + n + 1, :] = hi
            phi[base + 16 + n : base + 17 + n, :] = hi
            phi[base + 32 + n : base + 33 + n, :] = term - hi
    phi[96:97, :] = 1.0 - relax
    phit[...] = phi[...].T

    exact(f, 1, f)
    exact(q, 2, q)
    exact(jnp.where(ahead, before, after), 3, f)
    spread(1, [spread_f, scaled, reach])

    def sweep(r):
        rows = rows8(r)
        zero = jnp.zeros((8, 128), F32)
        ones = jnp.ones((8, 128), F32)

        def cols(t):
            return pl.ds(t * 128, 128)

        value = [[zero] * 3, [zero] * 3]
        rolls = [[zero, zero], [zero, zero]]
        f_near = [ones, ones]
        for step in range(16):
            for d in range(2):
                p = step if d == 0 else 15 - step
                f = [spread_f[d, rows, cols(3 * p + j)] for j in range(3)]
                first, second = (f[0], f[2]) if d == 0 else (f[2], f[0])
                near, far = first * f_near[d], second * first
                f_near[d] = second
                if d == 0:
                    gs = [near, jnp.where(low, near, far), far]
                else:
                    gs = [far, jnp.where(low, far, near), near]
                for j in (0, 1, 2) if d == 0 else (2, 1, 0):
                    t = 3 * p + j
                    s = scaled[d, rows, cols(t)] * val[d, rows, cols(t)]
                    two_off, one_off = rolls[d]
                    neighbour = jnp.where(low, two_off, one_off) if d == 0 else jnp.where(low, one_off, two_off)
                    rolls[d] = [one_off, pltpu.roll(s, 64, 1)]
                    value[d][j] = gs[j] * value[d][j] + (s + f[j] * neighbour)
                    val[d, rows, cols(t)] = value[d][j]

    def sweep_rows(r, _):
        sweep(r)
        return 0

    lax.fori_loop(0, 8, sweep_rows, 0)

    for t in range(1, NX):
        @pl.when(gx - t >= 0)
        def _():
            edge(0, t, (gx - t) % NX).wait_recv()

        @pl.when(gx + t < NX)
        def _():
            edge(1, t, (gx + t) % NX).wait_recv()

    def entering(d):
        def add(n, state):
            slot = gx - n - 1 if d == 0 else NX - 2 - gx - n
            products = rcv[d, slot, 0:8, :]
            through = [jnp.broadcast_to(products[:, r : r + 1], (8, 128)) for r in range(8)]
            new = []
            for r in range(8):
                new.append(through[r] * state[r] + rcv[d, slot, whole_row(r) : whole_row(r) + 8, :])
            for pair in range(4):
                mixed = jnp.where(low, through[pair], through[pair + 4])
                new.append(mixed * state[8 + pair] + rcv[d, slot, half_row(pair) : half_row(pair) + 8, :])
            return tuple(new)

        state = lax.fori_loop(0, gx if d == 0 else NX - 1 - gx, add, (jnp.zeros((8, 128), F32),) * 12)
        for pair in range(4):
            h = state[8 + pair]
            turned = pltpu.roll(h, 64, 1)
            for k in range(2):
                r = pair + 4 * k
                a = state[r]
                ra = pltpu.roll(a, 64, 1)
                at_low, at_high = (h, turned) if k == 0 else (turned, h)
                if d == 0:
                    tiles = (jnp.where(low, at_low, ra), jnp.where(low, ra, at_high), a)
                else:
                    tiles = (a, jnp.where(low, at_low, ra), jnp.where(low, ra, at_high))
                for j in range(3):
                    inc[d, 8 * r : 8 * r + 8, j * 128 : (j + 1) * 128] = tiles[j]

    entering(0)
    entering(1)

    weights = wmat[0:32, :].astype(BF16)

    def moments(slot, dst, dst_row):
        for half in range(2):
            cols = pl.ds(pl.multiple_of(slot * 768 + half * 384, 128), 384)
            swept = val[:, :, cols] + reach[:, :, cols] * inc[...]
            val[:, :, cols] = swept
            flat = swept.reshape(128, 384)
            hi = flat.astype(BF16)
            lo = (flat - hi.astype(F32)).astype(BF16)
            both = jnp.dot(weights, jnp.concatenate([hi, lo], axis=0), preferred_element_type=F32)
            total = both[0:16] + both[16:32]
            for j in range(3):
                dst[pl.ds(dst_row + (half * 3 + j) * 13, 13), :] = total[0:13, j * 128 : (j + 1) * 128]

    def slot_rows(n):
        return pl.ds(n * SLOT_ROWS, SLOT_ROWS)

    partner = vert_of(y, z, 1 - core)

    def to_slot(n):
        dy, dc = AWAY[n]
        target = vert_of((y + dy) % NY, z, (core + dc) % 2)
        return copy(stage.at[slot_rows(n), :], got.at[slot_rows(n), :], CR + n, CR + n, gx, target)

    for n, (dy, dc) in enumerate(AWAY):
        moments((core + dc) % 2 * 4 + (y + dy) % NY, stage if n < 7 else part, n % 7 * SLOT_ROWS)
        if n < 7:
            to_slot(n).start()
    for n in (6, 4, 5, 2, 3, 1, 0):
        to_slot(n).wait_recv()
        part[0:SLOT_ROWS, :] += got[slot_rows(n), :]

    def drain_sums():
        for n in range(7):
            to_slot(n).wait_send()

    def tile_rows(n):
        return pl.ds(pl.multiple_of(n * 16, 16), 16)

    mine = core * 4 + y
    own_row = (1 + mine) * SLOT_ROWS

    def to_z(n):
        peer = (z + n + 1) % NZ
        return copy(
            part.at[pl.ds(pl.multiple_of(peer * 16, 16), 16), :], got_z.at[tile_rows(n), :],
            ZR + n, ZR + n, gx, vert_of(y, peer, core),
        )

    def from_owner(n, owner, target):
        tile = pl.ds(pl.multiple_of(own_row + owner * 16, 16), 16)
        return copy(full.at[tile, :], full.at[tile, :], ZG + n, ZG + n, gx, vert_of(y, target, core))

    def drain_z():
        for n in range(7):
            @pl.when((z + n + 1) % NZ < OWNERS)
            def _():
                to_z(n).wait_send()

    far_first = (3, 2, 4, 1, 5, 0, 6)
    for n in far_first:
        @pl.when((z + n + 1) % NZ < OWNERS)
        def _():
            to_z(n).start()

    @pl.when(z < OWNERS)
    def _():
        total = part[pl.ds(pl.multiple_of(z * 16, 16), 16), :]
        for n in range(7):
            copy(got_z.at[tile_rows(n), :], got_z.at[tile_rows(n), :], ZR + n, ZR + n, gx, vert).wait_recv()
            total += got_z[tile_rows(n), :]
        full[pl.ds(pl.multiple_of(own_row + z * 16, 16), 16), :] = total
        for n in far_first:
            from_owner(n, z, (z + n + 1) % NZ).start()

    for n in range(7):
        owner = (z + NZ - n - 1) % NZ

        @pl.when(owner < OWNERS)
        def _():
            from_owner(n, owner, z).wait_recv()

    def slot_of(n):
        return pl.ds(pl.multiple_of((1 + n) * SLOT_ROWS, SLOT_ROWS), SLOT_ROWS)

    def gather(n, slot):
        dy, dc = AWAY[n]
        target = vert_of((y + dy) % NY, z, (core + dc) % 2)
        return copy(full.at[slot_of(slot), :], full.at[slot_of(slot), :], YG + n, YG + n, gx, target)

    def slot_from(n):
        dy, dc = AWAY[n]
        return (core + dc) % 2 * 4 + (y + NY - dy) % NY

    halo_slot = jnp.where(core == 1, -1, 8)

    def send_halo(n):
        return copy(
            full.at[slot_of(mine), :], full.at[slot_of(halo_slot), :], HALO + n, HALO,
            jnp.where(core == 1, gx + 1, gx - 1), vert_of((y + n) % NY, z, core),
        )

    def relay_halo(slot):
        return copy(full.at[slot_of(slot), :], full.at[slot_of(slot), :], CG, CG, gx, partner)

    @pl.when(halo_source)
    def _():
        for n in (2, 1, 3, 0):
            send_halo(n).start()

    for n in range(7):
        gather(n, mine).start()

    @pl.when(halo_here)
    def _():
        copy(full.at[slot_of(halo_slot), :], full.at[slot_of(halo_slot), :], HALO, HALO, gx, vert).wait_recv()
        relay_halo(halo_slot).start()

    nothing = jnp.zeros((SLOT_ROWS, 128), F32)

    @pl.when(jnp.logical_not(has_left))
    def _():
        full[slot_of(-1), :] = nothing

    @pl.when(jnp.logical_not(has_right))
    def _():
        full[slot_of(8), :] = nothing

    for n in range(7):
        gather(n, slot_from(n)).wait_recv()

    other_halo = jnp.where(core == 1, 8, -1)

    @pl.when(jnp.where(core == 1, has_right, has_left))
    def _():
        relay_halo(other_halo).wait_recv()

    for n in range(7):
        gather(n, mine).wait_send()

    @pl.when(halo_source)
    def _():
        for n in range(4):
            send_halo(n).wait_send()

    @pl.when(halo_here)
    def _():
        relay_halo(halo_slot).wait_send()

    @pl.when(z < OWNERS)
    def _():
        for n in range(7):
            from_owner(n, z, (z + n + 1) % NZ).wait_send()

    left_flag = jnp.where(has_left, 1.0, 0.0).astype(F32)
    right_flag = jnp.where(has_right, 1.0, 0.0).astype(F32)

    def smooth(src, dst, first, last, skip=0):
        def get(t):
            if t < 0 or t > 59:
                return [jnp.zeros((8, 128), F32)] * 2
            row = t // SLOT * SLOT_ROWS + t % SLOT * 13 if src is full else t * 16
            return [src[row + 8 * h : row + 8 * h + 8, :] for h in range(2)]

        def rolled(t):
            return [pltpu.roll(m, 64, 1) for m in get(t)]

        around = {t: rolled(t) for t in range(first - 2, first + 2)}
        for t in range(first, last + 1):
            around[t + 2] = rolled(t + 2)
            here = get(t)
            density = jnp.broadcast_to(here[0][0:1, :], (8, 128))
            coef = SMOOTH_RATE / (1.0 + density * density)
            if t < SLOT:
                coef = coef * left_flag
            if t >= 54:
                coef = coef * right_flag
            for h in range(2):
                before = jnp.where(low, around[t - 2][h], around[t - 1][h])
                after = jnp.where(low, around[t + 1][h], around[t + 2][h])
                dst[(t - skip) * 16 + 8 * h : (t - skip) * 16 + 8 * h + 8, :] = here[h] + coef * (before + after - 2.0 * here[h])
            del around[t - 2]

    smooth(full, tmp, 1, 58)
    smooth(tmp, again, 3, 56)
    smooth(again, tmp, 4, 55)
    smooth(tmp, moved, 6, 53, 6)
    drain_x()
    drain_sums()
    drain_z()


def relax_kernel(val, moved, phit, out, mac, mac_buf, coef_f, coef_l, keep, buf, out_sem, mac_sem):
    for t in range(TILES):
        mac_buf[:, t * 128 : (t + 1) * 128] = moved[t * 16 : t * 16 + 13, :]
    mac_copy = pltpu.make_async_copy(mac_buf, mac, mac_sem)
    mac_copy.start()

    def row(k):
        return jnp.tanh(moved[pl.ds(k, TILES, stride=16), :])

    density = 1.0 + 0.5 * row(0)
    ux, uy, uz = 0.5 * row(1), 0.5 * row(2), 0.5 * row(3)
    g = 1.0 / (1.0 + 0.5 * row(4))
    s0, s1, s2, s3, s4 = [0.2 * row(5 + j) for j in range(5)]
    qx, qy, qz = [0.2 * row(10 + j) for j in range(3)]
    front = density * g * jnp.sqrt(g)
    h = 0.5 * g
    sxx, syy = 0.5 * s3, 0.5 * s4
    szz = -(sxx + syy)
    square = ux * ux + uy * uy + uz * uz
    a = qx * ux + qy * uy + qz * uz
    b = h * square - 2.5
    ah = a * h
    scale = front * g
    quad = (
        ux * (sxx * ux + s0 * uy + s1 * uz) + uy * (syy * uy + s2 * uz) + szz * uz * uz
    )
    values_f = [
        scale * h * qx, scale * h * qy, scale * h * qz,
        scale * (sxx - g * qx * ux - ah),
        scale * (syy - g * qy * uy - ah),
        scale * (szz - g * qz * uz - ah),
        scale * (s0 - g * (qx * uy + qy * ux)),
        scale * (s1 - g * (qx * uz + qz * ux)),
        scale * (s2 - g * (qy * uz + qz * uy)),
        scale * (b * qx + 2.0 * ah * ux - (2.0 * sxx * ux + s0 * uy + s1 * uz)),
        scale * (b * qy + 2.0 * ah * uy - (s0 * ux + 2.0 * syy * uy + s2 * uz)),
        scale * (b * qz + 2.0 * ah * uz - (s1 * ux + s2 * uy + 2.0 * szz * uz)),
        front + scale * (quad - a * b),
    ]
    le = -LOG2E * h
    none = jnp.zeros_like(le)
    values_l = [none] * 3 + [le] * 3 + [none] * 3 + [-2.0 * le * ux, -2.0 * le * uy, -2.0 * le * uz, le * square]
    for n in range(16):
        coef_f[pl.ds(n, TILES, stride=16), :] = values_f[n] if n < 13 else none
        coef_l[pl.ds(n, TILES, stride=16), :] = values_l[n] if n < 13 else none

    lhs_f = phit[:, 0:48].astype(BF16)
    lhs_l = phit[:, 48:96].astype(BF16)
    keep[...] = jnp.broadcast_to(phit[:, 96:97], (128, 128))

    def split(ref, n):
        c = jnp.concatenate([ref[n * 96 + 16 * j : n * 96 + 16 * j + 16, :] for j in range(SLOT)], axis=1)
        hi = c.astype(BF16)
        lo = (c - hi.astype(F32)).astype(BF16)
        return jnp.concatenate([hi, lo, hi], axis=0)

    def put(n):
        return pltpu.make_async_copy(buf.at[n], out.at[:, :, n * 768 : (n + 1) * 768], out_sem.at[n])

    for n in range(8):
        poly = jnp.dot(lhs_f, split(coef_f, n), preferred_element_type=F32)
        power = jnp.dot(lhs_l, split(coef_l, n), preferred_element_type=F32)
        for j in range(SLOT):
            part = slice(j * 128, (j + 1) * 128)
            swept = val[:, :, n * 768 + j * 128 : n * 768 + (j + 1) * 128].reshape(128, 128)
            buf[n, :, :, part] = (keep[...] * swept + poly[:, part] * jnp.exp2(power[:, part])).reshape(2, 64, 128)
        put(n).start()
    for n in range(8):
        put(n).wait()
    mac_copy.wait()


def per_device(dist, factors, velocity, weights, relax):
    vmem = pl.BlockSpec(memory_space=pltpu.VMEM)
    hbm = pl.BlockSpec(memory_space=pltpu.HBM)
    operands = (dist, jnp.transpose(factors, (0, 2, 1)), velocity, weights, relax)
    swept, moved, phit = pl.pallas_call(
        kernel,
        out_shape=(
            jax.ShapeDtypeStruct((2, 64, 6144), F32),
            jax.ShapeDtypeStruct((TILES * 16, 128), F32),
            jax.ShapeDtypeStruct((128, 128), F32),
        ),
        in_specs=[hbm] * 5,
        out_specs=(vmem, vmem, vmem),
        scratch_shapes=[
            pltpu.VMEM((2, 32, 64), F32),
            pltpu.VMEM((3, 2, 64), F32),
            pltpu.VMEM((13, 2, 64), F32),
            pltpu.VMEM((2, 64), F32),
            pltpu.VMEM((96, 6144), BF16),
            pltpu.VMEM((512, 128), BF16),
            pltpu.VMEM((2, 64, 6144), F32),
            pltpu.VMEM((2, 64, 6144), F32),
            pltpu.VMEM((2, 64, 6144), F32),
            pltpu.VMEM((2, 104, 128), F32),
            pltpu.VMEM((2, 3, 104, 128), F32),
            pltpu.VMEM((2, 64, 384), F32),
            pltpu.VMEM((40, 256), F32),
            pltpu.VMEM((128, 128), F32),
            pltpu.VMEM((7 * SLOT_ROWS + 8, 128), F32),
            pltpu.VMEM((SLOT_ROWS + 8, 128), F32),
            pltpu.VMEM((7 * SLOT_ROWS, 128), F32),
            pltpu.VMEM((7 * 16, 128), F32),
            pltpu.VMEM((10 * SLOT_ROWS + 8, 128), F32),
            pltpu.VMEM((60 * 16, 128), F32),
            pltpu.VMEM((60 * 16, 128), F32),
            pltpu.SemaphoreType.DMA((8,)),
            pltpu.SemaphoreType.DMA((4,)),
            pltpu.SemaphoreType.DMA((N_SEM,)),
            pltpu.SemaphoreType.DMA((N_SEM,)),
        ],
        compiler_params=pltpu.CompilerParams(
            collective_id=0, has_side_effects=True, vmem_limit_bytes=40 * 2**20
        ),
    )(*[pltpu.with_memory_space_constraint(x, pltpu.HBM) for x in operands])
    return pl.pallas_call(
        relax_kernel,
        out_shape=(
            jax.ShapeDtypeStruct((2, 64, 6144), F32),
            jax.ShapeDtypeStruct((13, 6144), F32),
        ),
        in_specs=[vmem] * 3,
        out_specs=(hbm, hbm),
        scratch_shapes=[
            pltpu.VMEM((13, 6144), F32),
            pltpu.VMEM((TILES * 16, 128), F32),
            pltpu.VMEM((TILES * 16, 128), F32),
            pltpu.VMEM((128, 128), F32),
            pltpu.VMEM((8, 2, 64, 768), F32),
            pltpu.SemaphoreType.DMA((8,)),
            pltpu.SemaphoreType.DMA,
        ],
        compiler_params=pltpu.CompilerParams(vmem_limit_bytes=32 * 2**20),
    )(swept, moved, phit)


def solution(mesh):
    return jax.shard_map(
        per_device,
        mesh=mesh,
        in_specs=(
            P(None, "vert", "gx"),
            P(None, "vert", "gx"),
            P(None, None, "vert"),
            P(None, None, "vert"),
            P(None, "vert"),
        ),
        out_specs=(P(None, "vert", "gx"), P(None, "gx")),
        check_vma=False,
    )
```
